512 devices in a mesh: strip: 128 (over x, z_lo, y), branch: 4 (over z_hi, core).
Axes of the slice: x: 4, y: 8, z: 8 (z_hi: 2, z_lo: 4; z = z_hi * 4 + z_lo), core: 2. Of those that a mesh axis runs over, the one named last changes fastest.
Arguments:
- features: bfloat16 [1024, 192, 512], P('strip'), may hold values from -6 to 6
- cotangent: bfloat16 [1024, 192, 256], P('strip', None, 'branch'), may hold values from -6 to 6
- depth_weight: bfloat16 [4, 9, 512], P('branch'), may hold values from -2 to 2
- point_weight: bfloat16 [4, 512, 256], P('branch'), may hold values from -0.25 to 0.25
- joining_weight: bfloat16 [1024, 256], P('branch'), may hold values from -0.25 to 0.25
- branch_mask: int32 [4], replicated, may hold values from 0 to 1, as said below
Outputs:
- output: bfloat16 [1024, 192, 256], P('strip', None, 'branch')
- joining_grad: float32 [1024, 256], P('branch')
- point_grad: float32 [4, 512, 256], P('branch')
- depth_grad: float32 [4, 9, 512], P('branch')
The draws below stay inside these ranges and needn't reach their ends.
Inputs may be any that keep to these rules, and one draw needn't show every extreme that they name: `branch_mask`: 1 marks an active branch; at least one branch is active and at least one is not.
All inputs are finite; a program needn't handle non-finite values.
Results may differ from the reference program's by a relative error of at most 0.014.
Values may be sent and summed in bfloat16 or wider, within the bound.
A program may use at most 64 MiB of HBM per device.

```python
import math
import jax
import jax.numpy as jnp
from jax import lax

CIN = 512
CB = 256
DILATION_STEP = 6
WIDTH = 192
NB = 4
ROWS = 1024


def draw_branch_mask(key, part):
    first_key, second_key = jax.random.split(jax.random.fold_in(key, 7))
    order = jax.random.permutation(first_key, NB)
    active_count = jax.random.randint(second_key, (), 1, NB)
    return (order < active_count).astype(jnp.int32)


def shard_levels(stream_key, extent, cuts, least, top_value):
    level, own = 1.0, jax.random.fold_in(stream_key, 6)
    for axis_at, blocks in cuts:
        draws = jnp.exp(jax.random.uniform(jax.random.fold_in(own, axis_at), (blocks,), jnp.float32, least / len(cuts), top_value / len(cuts)))
        level = level * jnp.repeat(draws, extent[axis_at] // blocks).reshape([-1 if axis == axis_at else 1 for axis in range(len(extent))])
    return level


def centred(key, extent, width, limit, pieces=(), kind=jnp.bfloat16):
    result = width * jax.random.normal(key, extent, jnp.float32)
    if pieces:
        result = result * shard_levels(key, extent, pieces, -0.22, 0.18)
    return jnp.clip(result, -limit, limit).astype(kind)


def setup_inputs(seed: int = 0) -> dict:
    key_list = jax.random.split(jax.random.key(seed), 7)
    return {
        "features": centred(key_list[0], (ROWS, WIDTH, CIN), 1.0, 6.0, ((0, 128),)),
        "cotangent": centred(key_list[1], (ROWS, WIDTH, CB), 1.0, 6.0, ((0, 128), (2, 4))),
        "depth_weight": centred(key_list[2], (NB, 9, CIN), 9 ** -0.5, 2.0, ((0, 4),)),
        "point_weight": centred(key_list[3], (NB, CIN, CB), CIN ** -0.5, 0.25, ((0, 4),)),
        "joining_weight": centred(key_list[4], (NB * CB, CB), (2 * CB) ** -0.5, 0.25, ((0, 4),)),
        "branch_mask": draw_branch_mask(jax.random.fold_in(key_list[6], 71), 0),
    }


tanh_coef = 0.7978845608
cubic_coef = 0.044715
slope_coef = 0.134145

def gelu_tanh(values):
    inner = jnp.tanh(tanh_coef * (values + cubic_coef * values * values * values))
    return 0.5 * values * (1.0 + inner)

def gelu_slope(values):
    inner = jnp.tanh(tanh_coef * (values + cubic_coef * values * values * values))
    return 0.5 * (1.0 + inner) + 0.5 * values * (1.0 - inner * inner) * tanh_coef * (1.0 + slope_coef * values * values)

def contract_rows(left, right):
    return lax.dot_general(left, right, (((0,), (0,)), ((), ())), preferred_element_type=jnp.float32)

def contract_cols(left, right):
    return lax.dot_general(left, right, (((1,), (1,)), ((), ())), preferred_element_type=jnp.float32)

def tap_piece(padded, dilation_rate, tap_index, row_count, col_count):
    row_start = tap_index // 3 * dilation_rate
    col_start = tap_index % 3 * dilation_rate
    return padded[row_start:row_start + row_count, col_start:col_start + col_count, :]

def branch_apply_forward(features, depth_row, point_row, mask_value, dilation_rate):
    row_count, col_count, chan_count = features.shape
    padded = jnp.pad(features, ((dilation_rate, dilation_rate), (dilation_rate, dilation_rate), (0, 0)))
    kernel = depth_row.astype(jnp.float32)
    summed = jnp.zeros(features.shape, jnp.float32)
    for tap_index in range(9):
        piece = tap_piece(padded, dilation_rate, tap_index, row_count, col_count)
        summed = summed + piece.astype(jnp.float32) * kernel[tap_index]
    dw_out = summed.astype(jnp.bfloat16).reshape(row_count * col_count, chan_count)
    pre_act = jnp.dot(dw_out, point_row, preferred_element_type=jnp.float32)
    branch_out = (gelu_tanh(pre_act) * mask_value).astype(jnp.bfloat16)
    return (padded, dw_out, pre_act, branch_out)

def reference(features, cotangent, depth_weight, point_weight, joining_weight, branch_mask):
    row_count, col_count, chan_count = features.shape
    pixel_count = row_count * col_count
    out_width = cotangent.shape[2]
    pixel_scale = 1.0 / math.sqrt(pixel_count)
    mask_values = branch_mask.astype(jnp.float32)
    joined_sum = jnp.zeros((pixel_count, out_width), jnp.float32)
    for branch_slot in range(NB):
        dilation_rate = (branch_slot + 1) * DILATION_STEP
        results = branch_apply_forward(features, depth_weight[branch_slot], point_weight[branch_slot], mask_values[branch_slot], dilation_rate)
        weight_rows = joining_weight[branch_slot * CB:(branch_slot + 1) * CB]
        joined_sum = joined_sum + jnp.dot(results[3], weight_rows, preferred_element_type=jnp.float32)
    output = gelu_tanh(joined_sum).astype(jnp.bfloat16).reshape(row_count, col_count, out_width)
    grad_joined = (cotangent.reshape(pixel_count, out_width).astype(jnp.float32) * gelu_slope(joined_sum)).astype(jnp.bfloat16)
    joining_parts = []
    point_parts = []
    depth_parts = []
    for branch_slot in range(NB):
        dilation_rate = (branch_slot + 1) * DILATION_STEP
        padded, dw_out, pre_act, branch_out = branch_apply_forward(features, depth_weight[branch_slot], point_weight[branch_slot], mask_values[branch_slot], dilation_rate)
        weight_rows = joining_weight[branch_slot * CB:(branch_slot + 1) * CB]
        joining_parts.append(contract_rows(branch_out, grad_joined) * pixel_scale)
        grad_branch = contract_cols(grad_joined, weight_rows) * mask_values[branch_slot]
        grad_pre = (grad_branch * gelu_slope(pre_act)).astype(jnp.bfloat16)
        point_parts.append(contract_rows(dw_out, grad_pre) * pixel_scale)
        depthwise_gradient = contract_cols(grad_pre, point_weight[branch_slot]).reshape(row_count, col_count, chan_count)
        tap_sums = []
        for tap_index in range(9):
            piece = tap_piece(padded, dilation_rate, tap_index, row_count, col_count)
            tap_sums.append(lax.optimization_barrier(jnp.sum(depthwise_gradient * piece.astype(jnp.float32), axis=(0, 1))) * pixel_scale)
        depth_parts.append(jnp.stack(tap_sums))
    return (output, jnp.concatenate(joining_parts, 0), jnp.stack(point_parts), jnp.stack(depth_parts))
```

```python
import functools
import math

import jax
import jax.numpy as jnp
from jax import lax
from jax.experimental import pallas as pl
from jax.experimental.pallas import tpu as pltpu
from jax.sharding import PartitionSpec as P

DILATION_STEP = 6
HOPS = 3
MESH = pl.DeviceIdType.MESH

tanh_coef = 0.7978845608
cubic_coef = 0.044715
slope_coef = 0.134145


def gelu_tanh(values):
    inner = jnp.tanh(tanh_coef * (values + cubic_coef * values * values * values))
    return 0.5 * values * (1.0 + inner)


def gelu_slope(values):
    inner = jnp.tanh(tanh_coef * (values + cubic_coef * values * values * values))
    return 0.5 * (1.0 + inner) + 0.5 * values * (1.0 - inner * inner) * tanh_coef * (
        1.0 + slope_coef * values * values
    )


def contract_rows(left, right):
    return lax.dot_general(
        left, right, (((0,), (0,)), ((), ())), preferred_element_type=jnp.float32
    )


def contract_cols(left, right):
    return lax.dot_general(
        left, right, (((1,), (1,)), ((), ())), preferred_element_type=jnp.float32
    )


def tap_piece(padded, border_rows, dilation_rate, tap_index, row_count, col_count, chan_count):
    row_start = border_rows + (tap_index // 3 - 1) * dilation_rate
    col_start = border_rows + (tap_index % 3 - 1) * dilation_rate
    return lax.dynamic_slice(padded, (row_start, col_start, 0), (row_count, col_count, chan_count))


def greet(barrier, partners):
    for partner in partners:
        pl.semaphore_signal(barrier, inc=1, device_id=partner, device_id_type=MESH)
    pl.semaphore_wait(barrier, len(partners))


def strip_layout(strip_count):
    if strip_count == 128:
        return 4, 4, 8
    return {4: (2, 1, 2), 8: (2, 2, 2), 2: (2, 1, 1)}[strip_count]


def halo_kernel(strip_count, feat, ext, zeros, own_sem, zero_sem, send, recv, pass_send, pass_recv):
    rows = feat.shape[0]
    half = rows // 2
    strip = lax.axis_index("strip")
    branch = lax.axis_index("branch")
    core = lax.rem(branch, 2)
    sibling = branch + 1 - 2 * core
    after = lax.rem(strip + 1, strip_count)
    before = lax.rem(strip + strip_count - 1, strip_count)
    barrier = pltpu.get_barrier_semaphore()
    greet(barrier, [(after, branch), (before, branch), (strip, sibling)])

    centre = HOPS * rows
    own = pltpu.make_async_copy(feat, ext.at[pl.ds(centre, rows)], own_sem)
    own.start()

    def exists(offset):
        place = strip + offset
        return jnp.logical_and(place >= 0, place < strip_count)

    def place_of(offset, line, side):
        return centre + offset * rows + half * side + line

    def link_copy(way, step, line):
        at = 0 if way > 0 else 1
        target = after if way > 0 else before
        if step == 0:
            source = feat.at[pl.ds(half * core + line, 1)]
        else:
            source = ext.at[pl.ds(place_of(-way * step, line, core), 1)]
        return pltpu.make_async_remote_copy(
            src_ref=source,
            dst_ref=ext.at[pl.ds(place_of(-way * (step + 1), line, core), 1)],
            send_sem=send.at[at, step, line],
            recv_sem=recv.at[at, step, line],
            device_id=(target, branch),
            device_id_type=MESH,
        )

    def pass_copy(way, step, line, side):
        at = 0 if way > 0 else 1
        rows_at = ext.at[pl.ds(place_of(-way * (step + 1), line, side), 1)]
        return pltpu.make_async_remote_copy(
            src_ref=rows_at,
            dst_ref=rows_at,
            send_sem=pass_send.at[at, step, line],
            recv_sem=pass_recv.at[at, step, line],
            device_id=(strip, sibling),
            device_id_type=MESH,
        )

    every = [(step, line, way) for step in range(HOPS) for line in range(half) for way in (1, -1)]

    for step, line, way in every:
        if step == 0:

            @pl.when(exists(way))
            def _():
                link_copy(way, step, line).start()

    for offset in range(1, HOPS + 1):
        for way in (1, -1):

            @pl.when(jnp.logical_not(exists(offset * way)))
            def _():
                zeros[...] = jnp.zeros_like(zeros)
                fill = pltpu.make_async_copy(
                    zeros, ext.at[pl.ds(centre + offset * way * rows, rows)], zero_sem
                )
                fill.start()
                fill.wait()

    for step, line, way in every:

        @pl.when(exists(-way * (step + 1)))
        def _():
            link_copy(way, step, line).wait_recv()
            pass_copy(way, step, line, core).start()

        if step + 1 < HOPS:

            @pl.when(jnp.logical_and(exists(-way * (step + 1)), exists(way)))
            def _():
                link_copy(way, step + 1, line).start()

    for step, line, way in every:

        @pl.when(jnp.logical_and(exists(-way * step), exists(way)))
        def _():
            link_copy(way, step, line).wait_send()

        @pl.when(exists(-way * (step + 1)))
        def _():
            pass_copy(way, step, line, core).wait_send()
            pass_copy(way, step, line, 1 - core).wait_recv()

    own.wait()


def halo(features, strip_count):
    rows, cols, chans = features.shape
    half = rows // 2
    return pl.pallas_call(
        functools.partial(halo_kernel, strip_count),
        name="halo_rows",
        out_shape=jax.ShapeDtypeStruct(((2 * HOPS + 1) * rows, cols, chans), features.dtype),
        in_specs=[pl.BlockSpec(memory_space=pl.ANY)],
        out_specs=pl.BlockSpec(memory_space=pl.ANY),
        scratch_shapes=[
            pltpu.VMEM((rows, cols, chans), features.dtype),
            pltpu.SemaphoreType.DMA,
            pltpu.SemaphoreType.DMA,
            pltpu.SemaphoreType.DMA((2, HOPS, half)),
            pltpu.SemaphoreType.DMA((2, HOPS, half)),
            pltpu.SemaphoreType.DMA((2, HOPS, half)),
            pltpu.SemaphoreType.DMA((2, HOPS, half)),
        ],
        compiler_params=pltpu.CompilerParams(collective_id=0, has_side_effects=True),
    )(features)


CHUNKS = 3


def swap_halves(low, high):
    lane = lax.broadcasted_iota(jnp.int32, low.shape, 1)
    left = lane < 64
    return (
        jnp.where(left, low, pltpu.roll(high, 64, 1)),
        jnp.where(left, pltpu.roll(low, 64, 1), high),
    )


def join_kernel(
    branch_out, weight, cot, out, full_grad, blocks, total, near, far, away, grads,
    near_send, near_recv, far_send, far_recv, gfar_send, gfar_recv, gnear_send, gnear_recv,
):
    strip = lax.axis_index("strip")
    branch = lax.axis_index("branch")
    core = lax.rem(branch, 2)
    layer = branch // 2
    sibling = (strip, branch + 1 - 2 * core)
    across = (strip, branch + 2 - 4 * layer)
    barrier = pltpu.get_barrier_semaphore()
    greet(barrier, [sibling, across])
    pixels = branch_out.shape[0] // 2
    size = pixels // CHUNKS

    def span(chunk):
        return pl.ds(chunk * size, size)

    def remote(source, target, send_sem, recv_sem, device):
        return pltpu.make_async_remote_copy(
            src_ref=source, dst_ref=target, send_sem=send_sem, recv_sem=recv_sem,
            device_id=device, device_id_type=MESH,
        )

    def near_copy(chunk, side):
        return remote(
            blocks.at[2 * side + 1 - core, span(chunk)], near.at[side, span(chunk)],
            near_send.at[chunk, side], near_recv.at[chunk, side], sibling,
        )

    def far_copy(chunk):
        return remote(
            away.at[span(chunk)], far.at[span(chunk)], far_send.at[chunk], far_recv.at[chunk], across
        )

    def grad_far(chunk):
        spot = grads.at[branch, span(chunk)]
        return remote(spot, spot, gfar_send.at[chunk], gfar_recv.at[chunk], across)

    def grad_near(chunk, which, block):
        spot = grads.at[block, span(chunk)]
        return remote(spot, spot, gnear_send.at[chunk, which], gnear_recv.at[chunk, which], sibling)

    for chunk in range(CHUNKS):
        low = jnp.dot(branch_out[chunk * size:(chunk + 1) * size, :], weight[...], preferred_element_type=jnp.float32)
        high = jnp.dot(
            branch_out[pixels + chunk * size:pixels + (chunk + 1) * size, :], weight[...],
            preferred_element_type=jnp.float32,
        )
        for pair in range(2):
            first, second = swap_halves(
                low[:, 128 * pair:128 * (pair + 1)], high[:, 128 * pair:128 * (pair + 1)]
            )
            blocks[2 * pair, span(chunk), :] = first.astype(jnp.bfloat16)
            blocks[2 * pair + 1, span(chunk), :] = second.astype(jnp.bfloat16)
        for side in range(2):
            near_copy(chunk, side).start()

    for chunk in range(CHUNKS):
        for side in range(2):
            near_copy(chunk, side).wait_recv()
        there = 1 - layer
        away[span(chunk), :] = (
            blocks[2 * there + core, span(chunk), :].astype(jnp.float32)
            + near[there, span(chunk), :].astype(jnp.float32)
        ).astype(jnp.bfloat16)
        far_copy(chunk).start()
        total[span(chunk), :] = blocks[branch, span(chunk), :].astype(jnp.float32) + near[
            layer, span(chunk), :
        ].astype(jnp.float32)

    for chunk in range(CHUNKS):
        far_copy(chunk).wait_recv()
        joined = total[span(chunk), :] + far[span(chunk), :].astype(jnp.float32)
        inner = jnp.tanh(tanh_coef * (joined + cubic_coef * joined * joined * joined))
        slope = 0.5 * (1.0 + inner) + 0.5 * joined * (1.0 - inner * inner) * tanh_coef * (
            1.0 + slope_coef * joined * joined
        )
        grads[branch, span(chunk), :] = (cot[span(chunk), :].astype(jnp.float32) * slope).astype(
            jnp.bfloat16
        )
        grad_far(chunk).start()
        grad_near(chunk, 0, branch).start()
        out[span(chunk), :] = (0.5 * joined * (1.0 + inner)).astype(out.dtype)

    other = branch + 2 - 4 * layer
    beside = branch + 1 - 2 * core
    beside_other = other + 1 - 2 * core
    for chunk in range(CHUNKS):
        grad_far(chunk).wait_recv()
        grad_near(chunk, 1, other).start()
    for chunk in range(CHUNKS):
        grad_near(chunk, 0, beside).wait_recv()
        grad_near(chunk, 1, beside_other).wait_recv()
        for pair in range(2):
            low, high = swap_halves(
                grads[2 * pair, span(chunk), :].astype(jnp.float32),
                grads[2 * pair + 1, span(chunk), :].astype(jnp.float32),
            )
            full_grad[chunk * size:(chunk + 1) * size, 128 * pair:128 * (pair + 1)] = low.astype(jnp.bfloat16)
            full_grad[pixels + chunk * size:pixels + (chunk + 1) * size, 128 * pair:128 * (pair + 1)] = high.astype(
                jnp.bfloat16
            )

    for chunk in range(CHUNKS):
        for side in range(2):
            near_copy(chunk, side).wait_send()
        far_copy(chunk).wait_send()
        grad_far(chunk).wait_send()
        grad_near(chunk, 0, branch).wait_send()
        grad_near(chunk, 1, other).wait_send()


def join(branch_out, weight, cotangent):
    pixels, chans = branch_out.shape
    pixels = pixels // 2
    packed = jnp.concatenate([cotangent[:pixels], cotangent[pixels:]], axis=1)
    vmem = pl.BlockSpec(memory_space=pltpu.VMEM)
    out, full_grad = pl.pallas_call(
        join_kernel,
        name="joined_sum",
        out_shape=(
            jax.ShapeDtypeStruct((pixels, 128), jnp.bfloat16),
            jax.ShapeDtypeStruct((2 * pixels, chans), jnp.bfloat16),
        ),
        in_specs=[vmem] * 3,
        out_specs=(vmem, vmem),
        scratch_shapes=[
            pltpu.VMEM((4, pixels, 128), jnp.bfloat16),
            pltpu.VMEM((pixels, 128), jnp.float32),
            pltpu.VMEM((2, pixels, 128), jnp.bfloat16),
            pltpu.VMEM((pixels, 128), jnp.bfloat16),
            pltpu.VMEM((pixels, 128), jnp.bfloat16),
            pltpu.VMEM((4, pixels, 128), jnp.bfloat16),
            pltpu.SemaphoreType.DMA((CHUNKS, 2)),
            pltpu.SemaphoreType.DMA((CHUNKS, 2)),
            pltpu.SemaphoreType.DMA((CHUNKS,)),
            pltpu.SemaphoreType.DMA((CHUNKS,)),
            pltpu.SemaphoreType.DMA((CHUNKS,)),
            pltpu.SemaphoreType.DMA((CHUNKS,)),
            pltpu.SemaphoreType.DMA((CHUNKS, 2)),
            pltpu.SemaphoreType.DMA((CHUNKS, 2)),
        ],
        compiler_params=pltpu.CompilerParams(
            collective_id=1, has_side_effects=True, vmem_limit_bytes=32 << 20
        ),
    )(branch_out, weight, packed)
    output = jnp.concatenate([out[:, :64], out[:, 64:]], axis=0)
    return output, full_grad


def total_kernel(
    layout, piece, stored, scale, joining, point, depth, joining_out, point_out, depth_out,
    mine, from_x, from_y, from_z, gathered,
    x_send, x_recv, y_send, y_recv, z_send, z_recv, gy_send, gy_recv, gx_send, gx_recv,
):
    nx, nz, ny = layout
    strip = lax.axis_index("strip")
    branch = lax.axis_index("branch")
    y = lax.rem(strip, ny)
    z = lax.rem(strip // ny, nz)
    x = strip // (ny * nz)

    def x_peer(step):
        other = lax.rem(x + step, nx)
        return other, ((other * nz + z) * ny + y, branch)

    def y_peer(step):
        other = lax.rem(y + step, ny)
        return other, ((x * nz + z) * ny + other, branch)

    def z_peer(step):
        other = lax.rem(z + step, nz)
        return other, ((x * nz + other) * ny + y, branch)

    def remote(source, target, send_sem, recv_sem, device):
        return pltpu.make_async_remote_copy(
            src_ref=source, dst_ref=target, send_sem=send_sem, recv_sem=recv_sem,
            device_id=device, device_id_type=MESH,
        )

    barrier = pltpu.get_barrier_semaphore()
    greet(
        barrier,
        [x_peer(k)[1] for k in range(1, nx)]
        + [y_peer(k)[1] for k in range(1, ny)]
        + [z_peer(k)[1] for k in range(1, nz)],
    )

    per_half = nx * ny // 2
    pieces = []
    for lane_half in range(2):
        tables = [
            (joining, joining_out, 0, 256, 128 * lane_half),
            (point, point_out, 256, 768, 128 * lane_half),
            (depth, depth_out, 768, 784, 256 * lane_half),
            (depth, depth_out, 784, 800, 256 * lane_half + 128),
        ]
        for index in range(per_half):
            at = lane_half * per_half + index
            start, stop = index * piece, (index + 1) * piece
            for source, target, first, last, lane in tables:
                low, high = max(start, first), min(stop, last)
                if low < high:
                    pieces.append((at // ny, at % ny, low - start, high - start, source, target, low - first, high - first, lane))
            if stop > 800:
                pieces.append((at // ny, at % ny, max(800 - start, 0), piece, None, None, 0, 0, 0))
    for px, py, low, high, source, _, first, last, lane in pieces:
        if source is None:
            mine[px, py, low:high, :] = jnp.zeros((high - low, 128), jnp.float32)
        else:
            mine[px, py, low:high, :] = source[first:last, lane:lane + 128]

    def x_copy(step):
        other, device = x_peer(step)
        return remote(mine.at[other], from_x.at[step - 1], x_send.at[step - 1], x_recv.at[step - 1], device)

    for step in range(1, nx):
        x_copy(step).start()
    for step in range(1, nx):
        x_copy(step).wait_recv()
    summed = mine[x]
    for step in range(1, nx):
        summed = summed + from_x[step - 1]
    from_y[0] = summed

    def y_copy(step):
        other, device = y_peer(step)
        return remote(from_y.at[0, other], from_y.at[1, step - 1], y_send.at[step - 1], y_recv.at[step - 1], device)

    for step in range(1, ny):
        y_copy(step).start()
    for step in range(1, ny):
        y_copy(step).wait_recv()
    summed = from_y[0, y]
    for step in range(1, ny):
        summed = summed + from_y[1, step - 1]
    from_z[z] = summed

    def z_copy(step):
        spot = from_z.at[z]
        return remote(spot, spot, z_send.at[step - 1], z_recv.at[step - 1], z_peer(step)[1])

    for step in range(1, nz):
        z_copy(step).start()
    for step in range(1, nz):
        z_copy(step).wait_recv()
    summed = from_z[0]
    for other in range(1, nz):
        summed = summed + from_z[other]
    gathered[x, y, 0:piece, :] = (summed * scale).astype(jnp.bfloat16)
    if stored > piece:
        gathered[x, y, piece:stored, :] = jnp.zeros((stored - piece, 128), jnp.bfloat16)

    def gy_copy(step):
        spot = gathered.at[x, y]
        return remote(spot, spot, gy_send.at[step - 1], gy_recv.at[step - 1], y_peer(step)[1])

    for step in range(1, ny):
        gy_copy(step).start()
    for step in range(1, ny):
        gy_copy(step).wait_recv()

    def gx_copy(step):
        spot = gathered.at[x]
        return remote(spot, spot, gx_send.at[step - 1], gx_recv.at[step - 1], x_peer(step)[1])

    for step in range(1, nx):
        gx_copy(step).start()
    for step in range(1, nx):
        gx_copy(step).wait_recv()

    for px, py, low, high, source, target, first, last, lane in pieces:
        if source is not None:
            target[first:last, lane:lane + 128] = gathered[px, py, 0:piece, :].astype(jnp.float32)[low:high, :]

    for step in range(1, nx):
        x_copy(step).wait_send()
        gx_copy(step).wait_send()
    for step in range(1, ny):
        y_copy(step).wait_send()
        gy_copy(step).wait_send()
    for step in range(1, nz):
        z_copy(step).wait_send()


def weight_totals(joining, point, depth, scale, strip_count):
    nx, nz, ny = strip_layout(strip_count)
    piece = -(-1600 // (nx * ny) // 8) * 8
    stored = -(-piece // 16) * 16
    vmem = pl.BlockSpec(memory_space=pltpu.VMEM)
    dma = pltpu.SemaphoreType.DMA
    padded = jnp.concatenate([depth, jnp.zeros((16 - depth.shape[0], depth.shape[1]), jnp.float32)], 0)
    shapes = [joining.shape, point.shape, padded.shape]
    a, b, c = pl.pallas_call(
        functools.partial(total_kernel, (nx, nz, ny), piece, stored, scale),
        name="weight_totals",
        out_shape=tuple(jax.ShapeDtypeStruct(shape, jnp.float32) for shape in shapes),
        in_specs=[vmem] * 3,
        out_specs=(vmem,) * 3,
        scratch_shapes=[
            pltpu.VMEM((nx, ny, piece, 128), jnp.float32),
            pltpu.VMEM((max(nx - 1, 1), ny, piece, 128), jnp.float32),
            pltpu.VMEM((2, ny, piece, 128), jnp.float32),
            pltpu.VMEM((nz, piece, 128), jnp.float32),
            pltpu.VMEM((nx, ny, stored, 128), jnp.bfloat16),
            dma((nx,)), dma((nx,)), dma((ny,)), dma((ny,)), dma((nz,)), dma((nz,)),
            dma((ny,)), dma((ny,)), dma((nx,)), dma((nx,)),
        ],
        compiler_params=pltpu.CompilerParams(
            collective_id=2, has_side_effects=True, vmem_limit_bytes=32 << 20
        ),
    )(joining, point, padded)
    return a, b, c[: depth.shape[0]]


def per_device(features, cotangent, depth_weight, point_weight, joining_weight, branch_mask):
    row_count, col_count, chan_count = features.shape
    pixel_count = row_count * col_count
    strip_count = lax.axis_size("strip")
    branch_total = lax.axis_size("branch")
    local_branch = lax.axis_index("branch")
    dilation_rate = (local_branch + 1) * DILATION_STEP
    border_rows = branch_total * DILATION_STEP
    pixel_scale = 1.0 / math.sqrt(pixel_count * strip_count)
    active = jnp.sum(
        jnp.where(jnp.arange(branch_mask.shape[0]) == local_branch, branch_mask, 0)
    ).astype(jnp.float32)
    stacked = halo(features, strip_count)
    padded = jnp.pad(stacked, ((0, 0), (border_rows, border_rows), (0, 0)))
    kernel = depth_weight[0].astype(jnp.float32)
    summed = jnp.zeros(features.shape, jnp.float32)
    for tap_index in range(9):
        piece = tap_piece(
            padded, border_rows, dilation_rate, tap_index, row_count, col_count, chan_count
        )
        summed = summed + piece.astype(jnp.float32) * kernel[tap_index]
    dw_out = summed.astype(jnp.bfloat16).reshape(pixel_count, chan_count)
    pre_act = jnp.dot(dw_out, point_weight[0], preferred_element_type=jnp.float32)
    branch_out = (gelu_tanh(pre_act) * active).astype(jnp.bfloat16)
    own_width = cotangent.shape[2]
    output, full_grad = join(branch_out, joining_weight, cotangent.reshape(pixel_count, own_width))
    output = output.reshape(row_count, col_count, own_width)
    joining_part = contract_rows(branch_out, full_grad)
    grad_branch = contract_cols(full_grad, joining_weight) * active
    grad_pre = (grad_branch * gelu_slope(pre_act)).astype(jnp.bfloat16)
    point_part = contract_rows(dw_out, grad_pre)
    depthwise_gradient = contract_cols(grad_pre, point_weight[0]).reshape(
        row_count, col_count, chan_count
    )
    tap_sums = []
    for tap_index in range(9):
        piece = tap_piece(
            padded, border_rows, dilation_rate, tap_index, row_count, col_count, chan_count
        )
        tap_sums.append(jnp.sum(depthwise_gradient * piece.astype(jnp.float32), axis=(0, 1)))
    depth_part = jnp.stack(tap_sums)
    joining_total, point_total, depth_total = weight_totals(
        joining_part, point_part, depth_part, pixel_scale, strip_count
    )
    return (output, joining_total, point_total[None], depth_total[None])


def solution(mesh):
    placed = (
        P("strip", None, None),
        P("strip", None, "branch"),
        P("branch", None, None),
        P("branch", None, None),
        P("branch", None),
        P(),
    )
    return jax.shard_map(
        per_device,
        mesh=mesh,
        in_specs=placed,
        out_specs=(
            P("strip", None, "branch"),
            P("branch", None),
            P("branch", None, None),
            P("branch", None, None),
        ),
        check_vma=False,
    )
```

```python
import functools
import math

import jax
import jax.numpy as jnp
from jax import lax
from jax.experimental import pallas as pl
from jax.experimental.pallas import tpu as pltpu
from jax.sharding import PartitionSpec as P

DILATION_STEP = 6
HOPS = 3
MESH = pl.DeviceIdType.MESH

tanh_coef = 0.7978845608
cubic_coef = 0.044715
slope_coef = 0.134145


def contract_rows(left, right):
    return lax.dot_general(
        left, right, (((0,), (0,)), ((), ())), preferred_element_type=jnp.float32
    )


def contract_cols(left, right):
    return lax.dot_general(
        left, right, (((1,), (1,)), ((), ())), preferred_element_type=jnp.float32
    )


def greet(barrier, partners):
    for partner in partners:
        pl.semaphore_signal(barrier, inc=1, device_id=partner, device_id_type=MESH)
    pl.semaphore_wait(barrier, len(partners))


def strip_layout(strip_count):
    if strip_count == 128:
        return 4, 4, 8
    return {4: (2, 1, 2), 8: (2, 2, 2), 2: (2, 1, 1)}[strip_count]


CHUNKS = 4
LOW_ROWS = (2, 3, 0, 1)
HIGH_ROWS = (4, 5, 6, 7)
EDGE = 24


def swap_halves(low, high):
    lane = lax.broadcasted_iota(jnp.int32, low.shape, 1)
    left = lane < 64
    return (
        jnp.where(left, low, pltpu.roll(high, 64, 1)),
        jnp.where(left, pltpu.roll(low, 64, 1), high),
    )


def branch_kernel(
    strip_count, feat, cot, depth_w, point_w, join_w, active, out, join_part, point_part, depth_part,
    ext, taps, dw_out, slope, branch_out, blocks, near, away, far, total, grads, grad_dw,
    own_sem, send, recv, pass_send, pass_recv,
    near_send, near_recv, far_send, far_recv, gfar_send, gfar_recv, gnear_send, gnear_recv,
):
    rows, cols, chans = feat.shape
    half = rows // 2
    tiles = chans // 128
    strip = lax.axis_index("strip")
    branch = lax.axis_index("branch")
    core = lax.rem(branch, 2)
    layer = branch // 2
    rate = (branch + 1) * DILATION_STEP
    beside = branch + 1 - 2 * core
    other = branch + 2 - 4 * layer
    beside_other = other + 1 - 2 * core
    sibling = (strip, beside)
    across = (strip, other)
    after = (lax.rem(strip + 1, strip_count), branch)
    before = (lax.rem(strip + strip_count - 1, strip_count), branch)
    greet(pltpu.get_barrier_semaphore(), [after, before, sibling, across])

    def remote(source, target, send_sem, recv_sem, device):
        return pltpu.make_async_remote_copy(
            src_ref=source, dst_ref=target, send_sem=send_sem, recv_sem=recv_sem,
            device_id=device, device_id_type=MESH,
        )

    centre = HOPS * rows

    def exists(offset):
        place = strip + offset
        return jnp.logical_and(place >= 0, place < strip_count)

    def line_row(line, side):
        return side * HIGH_ROWS[line] + (1 - side) * LOW_ROWS[line]

    def link_copy(way, step, line):
        at = 0 if way > 0 else 1
        row = line_row(line, core)
        if step == 0:
            source = feat.at[pl.ds(row, 1)]
        else:
            source = ext.at[pl.ds(centre - way * step * rows + row, 1)]
        return remote(
            source, ext.at[pl.ds(centre - way * (step + 1) * rows + row, 1)],
            send.at[at, step, line], recv.at[at, step, line], after if way > 0 else before,
        )

    def pass_copy(way, step, line, side):
        at = 0 if way > 0 else 1
        spot = ext.at[pl.ds(centre - way * (step + 1) * rows + line_row(line, side), 1)]
        return remote(spot, spot, pass_send.at[at, step, line], pass_recv.at[at, step, line], sibling)

    ways = (1, -1)
    for line in range(half):
        for way in ways:

            @pl.when(exists(way))
            def _():
                link_copy(way, 0, line).start()

    own = pltpu.make_async_copy(feat, ext.at[pl.ds(centre, rows)], own_sem)
    own.start()

    for offset in range(1, HOPS + 1):
        for way in ways:

            @pl.when(jnp.logical_not(exists(offset * way)))
            def _():
                def fill(row, carry):
                    ext[centre + offset * way * rows + row] = jnp.zeros((cols, chans), ext.dtype)
                    return carry

                lax.fori_loop(0, rows, fill, 0)

    def clear(index, carry):
        for part in range(3):
            for tile in range(tiles):
                taps[index, part, tile, 0:EDGE, :] = jnp.zeros((EDGE, 128), jnp.float32)
                taps[index, part, tile, EDGE + cols:2 * EDGE + cols, :] = jnp.zeros((EDGE, 128), jnp.float32)
        return carry

    lax.fori_loop(0, rows, clear, 0)
    join_part[...] = jnp.zeros_like(join_part)
    point_part[...] = jnp.zeros_like(point_part)
    depth_part[...] = jnp.zeros_like(depth_part)

    def widen(row, part):
        at = centre + row + (part - 1) * rate
        for tile in range(tiles):
            taps[row, part, tile, EDGE:EDGE + cols, :] = ext[at, :, 128 * tile:128 * (tile + 1)].astype(jnp.float32)

    own.wait()

    def widen_own(row, carry):
        widen(row, 1)
        return carry

    lax.fori_loop(0, rows, widen_own, 0)

    def arrive(step, line):
        for way in ways:

            @pl.when(exists(-way * (step + 1)))
            def _():
                link_copy(way, step, line).wait_recv()

            if step + 1 < HOPS:

                @pl.when(jnp.logical_and(exists(-way * (step + 1)), exists(way)))
                def _():
                    link_copy(way, step + 1, line).start()

            @pl.when(exists(-way * (step + 1)))
            def _():
                pass_copy(way, step, line, core).start()

    def passed(step, line):
        for way in ways:

            @pl.when(exists(-way * (step + 1)))
            def _():
                pass_copy(way, step, line, 1 - core).wait_recv()

    def tap_columns(part):
        return pl.ds(EDGE + (part - 1) * rate, cols)

    def near_copy(chunk, side):
        return remote(
            blocks.at[2 * side + 1 - core, chunk], near.at[side, chunk],
            near_send.at[chunk, side], near_recv.at[chunk, side], sibling,
        )

    def far_copy(chunk):
        return remote(away.at[chunk], far.at[chunk], far_send.at[chunk], far_recv.at[chunk], across)

    def grad_far(chunk):
        spot = grads.at[branch, chunk]
        return remote(spot, spot, gfar_send.at[chunk], gfar_recv.at[chunk], across)

    def grad_near(chunk, which, block):
        spot = grads.at[block, chunk]
        return remote(spot, spot, gnear_send.at[chunk, which], gnear_recv.at[chunk, which], sibling)

    def forward(chunk):
        arrive(HOPS - 1, chunk)
        passed(HOPS - 1, chunk)
        for place, row in ((0, LOW_ROWS[chunk]), (1, HIGH_ROWS[chunk])):
            widen(row, 0)
            widen(row, 2)

            def depthwise(tile, carry):
                summed = jnp.zeros((cols, 128), jnp.float32)
                for part in range(9):
                    piece = taps[row, part // 3, tile, tap_columns(part % 3), :]
                    summed = summed + piece * depth_w[tile, part:part + 1, :]
                dw_out[chunk, place * cols:(place + 1) * cols, pl.ds(pl.multiple_of(tile * 128, 128), 128)] = (
                    summed.astype(jnp.bfloat16)
                )
                return carry

            lax.fori_loop(0, tiles, depthwise, 0)
        pre = jnp.dot(dw_out[chunk], point_w[...], preferred_element_type=jnp.float32)
        inner = jnp.tanh(tanh_coef * (pre + cubic_coef * pre * pre * pre))
        slope[chunk] = 0.5 * (1.0 + inner) + 0.5 * pre * (1.0 - inner * inner) * tanh_coef * (
            1.0 + slope_coef * pre * pre
        )
        branch_out[chunk] = (0.5 * pre * (1.0 + inner) * active[...]).astype(jnp.bfloat16)
        part_sum = jnp.dot(branch_out[chunk], join_w[...], preferred_element_type=jnp.float32)
        for pair in range(2):
            lanes = slice(128 * pair, 128 * (pair + 1))
            first, second = swap_halves(part_sum[:cols, lanes], part_sum[cols:, lanes])
            blocks[2 * pair, chunk] = first.astype(jnp.bfloat16)
            blocks[2 * pair + 1, chunk] = second.astype(jnp.bfloat16)
        for side in range(2):
            near_copy(chunk, side).start()

    def pair_sum(chunk):
        for side in range(2):
            near_copy(chunk, side).wait_recv()
        there = 1 - layer
        away[chunk] = (
            blocks[2 * there + core, chunk].astype(jnp.float32) + near[there, chunk].astype(jnp.float32)
        ).astype(jnp.bfloat16)
        far_copy(chunk).start()
        total[chunk] = blocks[branch, chunk].astype(jnp.float32) + near[layer, chunk].astype(jnp.float32)

    def finish_sum(chunk):
        far_copy(chunk).wait_recv()
        joined = total[chunk] + far[chunk].astype(jnp.float32)
        inner = jnp.tanh(tanh_coef * (joined + cubic_coef * joined * joined * joined))
        rise = 0.5 * (1.0 + inner) + 0.5 * joined * (1.0 - inner * inner) * tanh_coef * (
            1.0 + slope_coef * joined * joined
        )
        grads[branch, chunk] = (cot[chunk].astype(jnp.float32) * rise).astype(jnp.bfloat16)
        grad_far(chunk).start()
        grad_near(chunk, 0, branch).start()
        out[chunk] = (0.5 * joined * (1.0 + inner)).astype(out.dtype)

    def hand_on(chunk):
        grad_far(chunk).wait_recv()
        grad_near(chunk, 1, other).start()

    def backward(chunk):
        grad_near(chunk, 0, beside).wait_recv()
        grad_near(chunk, 1, beside_other).wait_recv()
        low_parts, high_parts = [], []
        for pair in range(2):
            low, high = swap_halves(
                grads[2 * pair, chunk].astype(jnp.float32), grads[2 * pair + 1, chunk].astype(jnp.float32)
            )
            low_parts.append(low)
            high_parts.append(high)
        full_grad = jnp.concatenate(
            [jnp.concatenate(low_parts, axis=1), jnp.concatenate(high_parts, axis=1)], axis=0
        ).astype(jnp.bfloat16)
        grad_branch = contract_cols(full_grad, join_w[...]) * active[...]
        grad_pre = (grad_branch * slope[chunk]).astype(jnp.bfloat16)
        grad_dw[...] = contract_cols(grad_pre, point_w[...])
        join_part[...] += contract_rows(branch_out[chunk], full_grad)
        point_part[...] += contract_rows(dw_out[chunk], grad_pre)
        for place, row in ((0, LOW_ROWS[chunk]), (1, HIGH_ROWS[chunk])):

            def depth_sums(tile, carry):
                here = grad_dw[place * cols:(place + 1) * cols, pl.ds(pl.multiple_of(tile * 128, 128), 128)]
                for part in range(9):
                    product = here * taps[row, part // 3, tile, tap_columns(part % 3), :]
                    depth_part[tile, part] += jnp.sum(product.reshape(cols // 8, 8, 128), axis=0)
                return carry

            lax.fori_loop(0, tiles, depth_sums, 0)

    for step in range(HOPS - 1):
        for line in range(half):
            arrive(step, line)
    for step in range(HOPS - 1):
        for line in range(half):
            passed(step, line)

    stages = (forward, pair_sum, finish_sum, hand_on, backward)
    for turn in range(CHUNKS + len(stages) - 1):
        for index, stage in enumerate(stages):
            if 0 <= turn - index < CHUNKS:
                stage(turn - index)

    for step in range(HOPS):
        for line in range(half):
            for way in ways:

                @pl.when(jnp.logical_and(exists(-way * step), exists(way)))
                def _():
                    link_copy(way, step, line).wait_send()

                @pl.when(exists(-way * (step + 1)))
                def _():
                    pass_copy(way, step, line, core).wait_send()

    for chunk in range(CHUNKS):
        for side in range(2):
            near_copy(chunk, side).wait_send()
        far_copy(chunk).wait_send()
        grad_far(chunk).wait_send()
        grad_near(chunk, 0, branch).wait_send()
        grad_near(chunk, 1, other).wait_send()


def branch_step(features, cotangent, depth_weight, point_weight, joining_weight, active, strip_count):
    rows, cols, chans = features.shape
    width = point_weight.shape[1]
    half = rows // 2
    tiles = chans // 128

    def lines(array, order):
        return jnp.concatenate([array[row:row + 1] for row in order], 0)

    packed = jnp.concatenate([lines(cotangent, LOW_ROWS), lines(cotangent, HIGH_ROWS)], axis=2)
    taps_weight = depth_weight.astype(jnp.float32).reshape(9, tiles, 128).transpose(1, 0, 2)
    vmem = pl.BlockSpec(memory_space=pltpu.VMEM)
    dma = pltpu.SemaphoreType.DMA
    low, wide = jnp.bfloat16, jnp.float32
    out, join_part, point_part, depth_part = pl.pallas_call(
        functools.partial(branch_kernel, strip_count),
        name="branch_step",
        out_shape=(
            jax.ShapeDtypeStruct((CHUNKS, cols, 128), low),
            jax.ShapeDtypeStruct((width, width), wide),
            jax.ShapeDtypeStruct((chans, width), wide),
            jax.ShapeDtypeStruct((tiles, 9, 8, 128), wide),
        ),
        in_specs=[pl.BlockSpec(memory_space=pl.ANY)] + [vmem] * 5,
        out_specs=(vmem,) * 4,
        scratch_shapes=[
            pltpu.VMEM(((2 * HOPS + 1) * rows, cols, chans), low),
            pltpu.VMEM((rows, 3, tiles, cols + 2 * EDGE, 128), wide),
            pltpu.VMEM((CHUNKS, 2 * cols, chans), low),
            pltpu.VMEM((CHUNKS, 2 * cols, width), wide),
            pltpu.VMEM((CHUNKS, 2 * cols, width), low),
            pltpu.VMEM((4, CHUNKS, cols, 128), low),
            pltpu.VMEM((2, CHUNKS, cols, 128), low),
            pltpu.VMEM((CHUNKS, cols, 128), low),
            pltpu.VMEM((CHUNKS, cols, 128), low),
            pltpu.VMEM((CHUNKS, cols, 128), wide),
            pltpu.VMEM((4, CHUNKS, cols, 128), low),
            pltpu.VMEM((2 * cols, chans), wide),
            dma,
            dma((2, HOPS, half)), dma((2, HOPS, half)), dma((2, HOPS, half)), dma((2, HOPS, half)),
            dma((CHUNKS, 2)), dma((CHUNKS, 2)), dma((CHUNKS,)), dma((CHUNKS,)),
            dma((CHUNKS,)), dma((CHUNKS,)), dma((CHUNKS, 2)), dma((CHUNKS, 2)),
        ],
        compiler_params=pltpu.CompilerParams(
            collective_id=0, has_side_effects=True, vmem_limit_bytes=52 << 20
        ),
    )(features, packed, taps_weight, point_weight, joining_weight, active)
    by_row = {}
    for chunk in range(CHUNKS):
        by_row[LOW_ROWS[chunk]] = out[chunk:chunk + 1, :, :64]
        by_row[HIGH_ROWS[chunk]] = out[chunk:chunk + 1, :, 64:]
    output = jnp.concatenate([by_row[row] for row in range(rows)], 0)
    return output, join_part, point_part, depth_part


def total_kernel(
    layout, piece, stored, scale, joining, point, depth, joining_out, point_out, depth_out,
    depth_rows, mine, from_x, from_y, from_z, gathered,
    x_send, x_recv, y_send, y_recv, z_send, z_recv, gy_send, gy_recv, gx_send, gx_recv,
):
    nx, nz, ny = layout
    strip = lax.axis_index("strip")
    branch = lax.axis_index("branch")
    y = lax.rem(strip, ny)
    z = lax.rem(strip // ny, nz)
    x = strip // (ny * nz)

    def x_peer(step):
        other = lax.rem(x + step, nx)
        return other, ((other * nz + z) * ny + y, branch)

    def y_peer(step):
        other = lax.rem(y + step, ny)
        return other, ((x * nz + z) * ny + other, branch)

    def z_peer(step):
        other = lax.rem(z + step, nz)
        return other, ((x * nz + other) * ny + y, branch)

    def remote(source, target, send_sem, recv_sem, device):
        return pltpu.make_async_remote_copy(
            src_ref=source, dst_ref=target, send_sem=send_sem, recv_sem=recv_sem,
            device_id=device, device_id_type=MESH,
        )

    barrier = pltpu.get_barrier_semaphore()
    greet(
        barrier,
        [x_peer(k)[1] for k in range(1, nx)]
        + [y_peer(k)[1] for k in range(1, ny)]
        + [z_peer(k)[1] for k in range(1, nz)],
    )

    depth_rows[...] = jnp.zeros_like(depth_rows)
    for tile in range(depth.shape[0]):
        for part in range(depth.shape[1]):
            depth_rows[part:part + 1, 128 * tile:128 * (tile + 1)] = jnp.sum(depth[tile, part], axis=0, keepdims=True)

    per_half = nx * ny // 2
    pieces = []
    for lane_half in range(2):
        tables = [
            (joining, joining_out, 0, 256, 128 * lane_half),
            (point, point_out, 256, 768, 128 * lane_half),
            (depth_rows, depth_out, 768, 784, 256 * lane_half),
            (depth_rows, depth_out, 784, 800, 256 * lane_half + 128),
        ]
        for index in range(per_half):
            at = lane_half * per_half + index
            start, stop = index * piece, (index + 1) * piece
            for source, target, first, last, lane in tables:
                low, high = max(start, first), min(stop, last)
                if low < high:
                    pieces.append((at // ny, at % ny, low - start, high - start, source, target, low - first, high - first, lane))
            if stop > 800:
                pieces.append((at // ny, at % ny, max(800 - start, 0), piece, None, None, 0, 0, 0))
    for px, py, low, high, source, _, first, last, lane in pieces:
        if source is None:
            mine[px, py, low:high, :] = jnp.zeros((high - low, 128), jnp.float32)
        else:
            mine[px, py, low:high, :] = source[first:last, lane:lane + 128]

    def x_copy(step):
        other, device = x_peer(step)
        return remote(mine.at[other], from_x.at[step - 1], x_send.at[step - 1], x_recv.at[step - 1], device)

    for step in range(1, nx):
        x_copy(step).start()
    for step in range(1, nx):
        x_copy(step).wait_recv()
    summed = mine[x]
    for step in range(1, nx):
        summed = summed + from_x[step - 1]
    from_y[0] = summed

    def y_copy(step):
        other, device = y_peer(step)
        return remote(from_y.at[0, other], from_y.at[1, step - 1], y_send.at[step - 1], y_recv.at[step - 1], device)

    for step in range(1, ny):
        y_copy(step).start()
    for step in range(1, ny):
        y_copy(step).wait_recv()
    summed = from_y[0, y]
    for step in range(1, ny):
        summed = summed + from_y[1, step - 1]
    from_z[z] = summed

    def z_copy(step):
        spot = from_z.at[z]
        return remote(spot, spot, z_send.at[step - 1], z_recv.at[step - 1], z_peer(step)[1])

    for step in range(1, nz):
        z_copy(step).start()
    for step in range(1, nz):
        z_copy(step).wait_recv()
    summed = from_z[0]
    for other in range(1, nz):
        summed = summed + from_z[other]
    gathered[x, y, 0:piece, :] = (summed * scale).astype(jnp.bfloat16)
    if stored > piece:
        gathered[x, y, piece:stored, :] = jnp.zeros((stored - piece, 128), jnp.bfloat16)

    def gy_copy(step):
        spot = gathered.at[x, y]
        return remote(spot, spot, gy_send.at[step - 1], gy_recv.at[step - 1], y_peer(step)[1])

    for step in range(1, ny):
        gy_copy(step).start()
    for step in range(1, ny):
        gy_copy(step).wait_recv()

    def gx_copy(step):
        spot = gathered.at[x]
        return remote(spot, spot, gx_send.at[step - 1], gx_recv.at[step - 1], x_peer(step)[1])

    for step in range(1, nx):
        gx_copy(step).start()
    for step in range(1, nx):
        gx_copy(step).wait_recv()

    for px, py, low, high, source, target, first, last, lane in pieces:
        if source is not None:
            target[first:last, lane:lane + 128] = gathered[px, py, 0:piece, :].astype(jnp.float32)[low:high, :]

    for step in range(1, nx):
        x_copy(step).wait_send()
        gx_copy(step).wait_send()
    for step in range(1, ny):
        y_copy(step).wait_send()
        gy_copy(step).wait_send()
    for step in range(1, nz):
        z_copy(step).wait_send()


def weight_totals(joining, point, depth, scale, strip_count):
    nx, nz, ny = strip_layout(strip_count)
    piece = -(-1600 // (nx * ny) // 8) * 8
    stored = -(-piece // 16) * 16
    vmem = pl.BlockSpec(memory_space=pltpu.VMEM)
    dma = pltpu.SemaphoreType.DMA
    depth_shape = (16, depth.shape[0] * 128)
    shapes = [joining.shape, point.shape, depth_shape]
    a, b, c = pl.pallas_call(
        functools.partial(total_kernel, (nx, nz, ny), piece, stored, scale),
        name="weight_totals",
        out_shape=tuple(jax.ShapeDtypeStruct(shape, jnp.float32) for shape in shapes),
        in_specs=[vmem] * 3,
        out_specs=(vmem,) * 3,
        scratch_shapes=[
            pltpu.VMEM(depth_shape, jnp.float32),
            pltpu.VMEM((nx, ny, piece, 128), jnp.float32),
            pltpu.VMEM((max(nx - 1, 1), ny, piece, 128), jnp.float32),
            pltpu.VMEM((2, ny, piece, 128), jnp.float32),
            pltpu.VMEM((nz, piece, 128), jnp.float32),
            pltpu.VMEM((nx, ny, stored, 128), jnp.bfloat16),
            dma((nx,)), dma((nx,)), dma((ny,)), dma((ny,)), dma((nz,)), dma((nz,)),
            dma((ny,)), dma((ny,)), dma((nx,)), dma((nx,)),
        ],
        compiler_params=pltpu.CompilerParams(
            collective_id=1, has_side_effects=True, vmem_limit_bytes=32 << 20
        ),
    )(joining, point, depth)
    return a, b, c[: depth.shape[1]]


def per_device(features, cotangent, depth_weight, point_weight, joining_weight, branch_mask):
    row_count, col_count, chan_count = features.shape
    strip_count = lax.axis_size("strip")
    local_branch = lax.axis_index("branch")
    pixel_scale = 1.0 / math.sqrt(row_count * col_count * strip_count)
    active = jnp.sum(
        jnp.where(jnp.arange(branch_mask.shape[0]) == local_branch, branch_mask, 0)
    ).astype(jnp.float32)
    active = jnp.full((1, point_weight.shape[2]), active)
    output, joining_part, point_part, depth_part = branch_step(
        features, cotangent, depth_weight[0], point_weight[0], joining_weight, active, strip_count
    )
    joining_total, point_total, depth_total = weight_totals(
        joining_part, point_part, depth_part, pixel_scale, strip_count
    )
    return (output, joining_total, point_total[None], depth_total[None])


def solution(mesh):
    placed = (
        P("strip", None, None),
        P("strip", None, "branch"),
        P("branch", None, None),
        P("branch", None, None),
        P("branch", None),
        P(),
    )
    return jax.shard_map(
        per_device,
        mesh=mesh,
        in_specs=placed,
        out_specs=(
            P("strip", None, "branch"),
            P("branch", None),
            P("branch", None, None),
            P("branch", None, None),
        ),
        check_vma=False,
    )
```

```python
import functools
import math

import jax
import jax.numpy as jnp
from jax import lax
from jax.experimental import pallas as pl
from jax.experimental.pallas import tpu as pltpu
from jax.sharding import PartitionSpec as P

DILATION_STEP = 6
HOPS = 3
MESH = pl.DeviceIdType.MESH

tanh_coef = 0.7978845608
cubic_coef = 0.044715
slope_coef = 0.134145


def contract_rows(left, right):
    return lax.dot_general(
        left, right, (((0,), (0,)), ((), ())), preferred_element_type=jnp.float32
    )


def contract_cols(left, right):
    return lax.dot_general(
        left, right, (((1,), (1,)), ((), ())), preferred_element_type=jnp.float32
    )


def greet(barrier, partners):
    for partner in partners:
        pl.semaphore_signal(barrier, inc=1, device_id=partner, device_id_type=MESH)
    pl.semaphore_wait(barrier, len(partners))


def strip_layout(strip_count):
    if strip_count == 128:
        return 4, 4, 8
    return {4: (2, 1, 2), 8: (2, 2, 2), 2: (2, 1, 1)}[strip_count]


CHUNKS = 4
LOW_ROWS = (2, 0, 3, 1)
HIGH_ROWS = (4, 6, 5, 7)
EDGE = 24


def swap_halves(low, high):
    lane = lax.broadcasted_iota(jnp.int32, low.shape, 1)
    left = lane < 64
    return (
        jnp.where(left, low, pltpu.roll(high, 64, 1)),
        jnp.where(left, pltpu.roll(low, 64, 1), high),
    )


def branch_kernel(
    strip_count, feat, cot, depth_w, point_w, join_w, mask, out, join_part, point_part, depth_part,
    ext, taps, dw_out, slope, branch_out, blocks, near, away, far, total, grads, grad_dw,
    own_sem, send, recv, pass_send, pass_recv,
    near_send, near_recv, far_send, far_recv, gfar_send, gfar_recv, gnear_send, gnear_recv,
):
    rows, cols, chans = feat.shape
    half = rows // 2
    tiles = chans // 128
    strip = lax.axis_index("strip")
    branch = lax.axis_index("branch")
    core = lax.rem(branch, 2)
    layer = branch // 2
    rate = (branch + 1) * DILATION_STEP
    beside = branch + 1 - 2 * core
    other = branch + 2 - 4 * layer
    beside_other = other + 1 - 2 * core
    sibling = (strip, beside)
    across = (strip, other)
    after = (lax.rem(strip + 1, strip_count), branch)
    before = (lax.rem(strip + strip_count - 1, strip_count), branch)
    active = mask[branch].astype(jnp.float32)
    greet(pltpu.get_barrier_semaphore(), [after, before, sibling, across])

    def remote(source, target, send_sem, recv_sem, device):
        return pltpu.make_async_remote_copy(
            src_ref=source, dst_ref=target, send_sem=send_sem, recv_sem=recv_sem,
            device_id=device, device_id_type=MESH,
        )

    centre = HOPS * rows

    def exists(offset):
        place = strip + offset
        return jnp.logical_and(place >= 0, place < strip_count)

    def line_row(line, side):
        return side * HIGH_ROWS[line] + (1 - side) * LOW_ROWS[line]

    def link_copy(way, step, line):
        at = 0 if way > 0 else 1
        row = line_row(line, core)
        if step == 0:
            source = feat.at[pl.ds(row, 1)]
        else:
            source = ext.at[pl.ds(centre - way * step * rows + row, 1)]
        return remote(
            source, ext.at[pl.ds(centre - way * (step + 1) * rows + row, 1)],
            send.at[at, step, line], recv.at[at, step, line], after if way > 0 else before,
        )

    def pass_copy(way, step, line, side):
        at = 0 if way > 0 else 1
        spot = ext.at[pl.ds(centre - way * (step + 1) * rows + line_row(line, side), 1)]
        return remote(spot, spot, pass_send.at[at, step, line], pass_recv.at[at, step, line], sibling)

    ways = (1, -1)

    def send_own(line):
        for way in ways:

            @pl.when(exists(way))
            def _():
                link_copy(way, 0, line).start()

    send_own(0)
    send_own(1)
    own = pltpu.make_async_copy(feat, ext.at[pl.ds(centre, rows)], own_sem)
    own.start()

    for offset in range(1, HOPS + 1):
        for way in ways:

            @pl.when(jnp.logical_not(exists(offset * way)))
            def _():
                def fill(row, carry):
                    ext[centre + offset * way * rows + row] = jnp.zeros((cols, chans), ext.dtype)
                    return carry

                lax.fori_loop(0, rows, fill, 0)

    def clear(index, carry):
        for part in range(3):
            for tile in range(tiles):
                taps[index, part, tile, 0:EDGE, :] = jnp.zeros((EDGE, 128), jnp.float32)
                taps[index, part, tile, EDGE + cols:2 * EDGE + cols, :] = jnp.zeros((EDGE, 128), jnp.float32)
        return carry

    lax.fori_loop(0, rows, clear, 0)
    join_part[...] = jnp.zeros_like(join_part)
    point_part[...] = jnp.zeros_like(point_part)
    depth_part[...] = jnp.zeros_like(depth_part)

    def widen(row, part):
        at = centre + row + (part - 1) * rate
        for tile in range(tiles):
            taps[row, part, tile, EDGE:EDGE + cols, :] = ext[at, :, 128 * tile:128 * (tile + 1)].astype(jnp.float32)

    own.wait()

    def widen_own(row, carry):
        widen(row, 1)
        return carry

    lax.fori_loop(0, rows, widen_own, 0)

    def arrive(step, line):
        for way in ways:

            @pl.when(exists(-way * (step + 1)))
            def _():
                link_copy(way, step, line).wait_recv()

            if step + 1 < HOPS:

                @pl.when(jnp.logical_and(exists(-way * (step + 1)), exists(way)))
                def _():
                    link_copy(way, step + 1, line).start()

            @pl.when(exists(-way * (step + 1)))
            def _():
                pass_copy(way, step, line, core).start()

    def passed(step, line):
        for way in ways:

            @pl.when(exists(-way * (step + 1)))
            def _():
                pass_copy(way, step, line, 1 - core).wait_recv()

    def tap_columns(part):
        return pl.ds(EDGE + (part - 1) * rate, cols)

    def near_copy(chunk, side):
        return remote(
            blocks.at[2 * side + 1 - core, chunk], near.at[side, chunk],
            near_send.at[chunk, side], near_recv.at[chunk, side], sibling,
        )

    def far_copy(chunk):
        return remote(away.at[chunk], far.at[chunk], far_send.at[chunk], far_recv.at[chunk], across)

    def grad_far(chunk):
        spot = grads.at[branch, chunk]
        return remote(spot, spot, gfar_send.at[chunk], gfar_recv.at[chunk], across)

    def grad_near(chunk, which, block):
        spot = grads.at[block, chunk]
        return remote(spot, spot, gnear_send.at[chunk, which], gnear_recv.at[chunk, which], sibling)

    def forward(chunk):
        arrive(HOPS - 1, chunk)
        passed(HOPS - 1, chunk)
        for place, row in ((0, LOW_ROWS[chunk]), (1, HIGH_ROWS[chunk])):
            widen(row, 0)
            widen(row, 2)

            def depthwise(tile, carry):
                lanes = pl.ds(pl.multiple_of(tile * 128, 128), 128)
                weights = depth_w[0, :, lanes].astype(jnp.float32)
                summed = jnp.zeros((cols, 128), jnp.float32)
                for part in range(9):
                    piece = taps[row, part // 3, tile, tap_columns(part % 3), :]
                    summed = summed + piece * weights[part:part + 1, :]
                dw_out[chunk, place * cols:(place + 1) * cols, lanes] = summed.astype(jnp.bfloat16)
                return carry

            lax.fori_loop(0, tiles, depthwise, 0)
        pre = jnp.dot(dw_out[chunk], point_w[0], preferred_element_type=jnp.float32)
        inner = jnp.tanh(tanh_coef * (pre + cubic_coef * pre * pre * pre))
        slope[chunk] = 0.5 * (1.0 + inner) + 0.5 * pre * (1.0 - inner * inner) * tanh_coef * (
            1.0 + slope_coef * pre * pre
        )
        branch_out[chunk] = (0.5 * pre * (1.0 + inner) * active).astype(jnp.bfloat16)
        part_sum = jnp.dot(branch_out[chunk], join_w[...], preferred_element_type=jnp.float32)
        for pair in range(2):
            lanes = slice(128 * pair, 128 * (pair + 1))
            first, second = swap_halves(part_sum[:cols, lanes], part_sum[cols:, lanes])
            blocks[2 * pair, chunk] = first.astype(jnp.bfloat16)
            blocks[2 * pair + 1, chunk] = second.astype(jnp.bfloat16)
        for side in range(2):
            near_copy(chunk, side).start()

    def pair_sum(chunk):
        for side in range(2):
            near_copy(chunk, side).wait_recv()
        there = 1 - layer
        away[chunk] = (
            blocks[2 * there + core, chunk].astype(jnp.float32) + near[there, chunk].astype(jnp.float32)
        ).astype(jnp.bfloat16)
        far_copy(chunk).start()
        total[chunk] = blocks[branch, chunk].astype(jnp.float32) + near[layer, chunk].astype(jnp.float32)

    def finish_sum(chunk):
        far_copy(chunk).wait_recv()
        joined = total[chunk] + far[chunk].astype(jnp.float32)
        inner = jnp.tanh(tanh_coef * (joined + cubic_coef * joined * joined * joined))
        rise = 0.5 * (1.0 + inner) + 0.5 * joined * (1.0 - inner * inner) * tanh_coef * (
            1.0 + slope_coef * joined * joined
        )
        low_row, high_row = LOW_ROWS[chunk], HIGH_ROWS[chunk]
        given = jnp.concatenate([cot[low_row].astype(jnp.float32), cot[high_row].astype(jnp.float32)], axis=1)
        grads[branch, chunk] = (given * rise).astype(jnp.bfloat16)
        grad_far(chunk).start()
        grad_near(chunk, 0, branch).start()
        result = (0.5 * joined * (1.0 + inner)).astype(out.dtype)
        out[low_row] = result[:, :64]
        out[high_row] = result[:, 64:]

    def hand_on(chunk):
        grad_far(chunk).wait_recv()
        grad_near(chunk, 1, other).start()

    def backward(chunk):
        grad_near(chunk, 0, beside).wait_recv()
        grad_near(chunk, 1, beside_other).wait_recv()
        low_parts, high_parts = [], []
        for pair in range(2):
            low, high = swap_halves(
                grads[2 * pair, chunk].astype(jnp.float32), grads[2 * pair + 1, chunk].astype(jnp.float32)
            )
            low_parts.append(low)
            high_parts.append(high)
        full_grad = jnp.concatenate(
            [jnp.concatenate(low_parts, axis=1), jnp.concatenate(high_parts, axis=1)], axis=0
        ).astype(jnp.bfloat16)
        grad_branch = contract_cols(full_grad, join_w[...]) * active
        grad_pre = (grad_branch * slope[chunk]).astype(jnp.bfloat16)
        grad_dw[...] = contract_cols(grad_pre, point_w[0])
        join_part[...] += contract_rows(branch_out[chunk], full_grad)
        point_part[...] += contract_rows(dw_out[chunk], grad_pre)
        for place, row in ((0, LOW_ROWS[chunk]), (1, HIGH_ROWS[chunk])):

            def depth_sums(tile, carry):
                here = grad_dw[place * cols:(place + 1) * cols, pl.ds(pl.multiple_of(tile * 128, 128), 128)]
                for part in range(9):
                    product = here * taps[row, part // 3, tile, tap_columns(part % 3), :]
                    depth_part[tile, part] += jnp.sum(product.reshape(cols // 8, 8, 128), axis=0)
                return carry

            lax.fori_loop(0, tiles, depth_sums, 0)

    for step in range(HOPS - 1):
        for line in (0, 1):
            arrive(step, line)
    send_own(2)
    send_own(3)
    for step in range(HOPS - 1):
        for line in (0, 1):
            passed(step, line)
    forward(0)
    pair_sum(0)
    forward(1)
    finish_sum(0)
    pair_sum(1)
    arrive(0, 2)
    hand_on(0)
    finish_sum(1)
    arrive(0, 3)
    backward(0)
    hand_on(1)
    arrive(1, 2)
    backward(1)
    arrive(1, 3)
    for step in range(HOPS - 1):
        for line in (2, 3):
            passed(step, line)
    forward(2)
    pair_sum(2)
    forward(3)
    finish_sum(2)
    pair_sum(3)
    hand_on(2)
    finish_sum(3)
    backward(2)
    hand_on(3)
    backward(3)

    for step in range(HOPS):
        for line in range(half):
            for way in ways:

                @pl.when(jnp.logical_and(exists(-way * step), exists(way)))
                def _():
                    link_copy(way, step, line).wait_send()

                @pl.when(exists(-way * (step + 1)))
                def _():
                    pass_copy(way, step, line, core).wait_send()

    for chunk in range(CHUNKS):
        for side in range(2):
            near_copy(chunk, side).wait_send()
        far_copy(chunk).wait_send()
        grad_far(chunk).wait_send()
        grad_near(chunk, 0, branch).wait_send()
        grad_near(chunk, 1, other).wait_send()


def branch_step(features, cotangent, depth_weight, point_weight, joining_weight, branch_mask, strip_count):
    rows, cols, chans = features.shape
    width = point_weight.shape[2]
    half = rows // 2
    tiles = chans // 128
    vmem = pl.BlockSpec(memory_space=pltpu.VMEM)
    dma = pltpu.SemaphoreType.DMA
    low, wide = jnp.bfloat16, jnp.float32
    return pl.pallas_call(
        functools.partial(branch_kernel, strip_count),
        name="branch_step",
        out_shape=(
            jax.ShapeDtypeStruct(cotangent.shape, low),
            jax.ShapeDtypeStruct((width, width), wide),
            jax.ShapeDtypeStruct((chans, width), wide),
            jax.ShapeDtypeStruct((tiles, 9, 8, 128), wide),
        ),
        in_specs=[pl.BlockSpec(memory_space=pl.ANY)] + [vmem] * 4 + [pl.BlockSpec(memory_space=pltpu.SMEM)],
        out_specs=(vmem,) * 4,
        scratch_shapes=[
            pltpu.VMEM(((2 * HOPS + 1) * rows, cols, chans), low),
            pltpu.VMEM((rows, 3, tiles, cols + 2 * EDGE, 128), wide),
            pltpu.VMEM((CHUNKS, 2 * cols, chans), low),
            pltpu.VMEM((CHUNKS, 2 * cols, width), wide),
            pltpu.VMEM((CHUNKS, 2 * cols, width), low),
            pltpu.VMEM((4, CHUNKS, cols, 128), low),
            pltpu.VMEM((2, CHUNKS, cols, 128), low),
            pltpu.VMEM((CHUNKS, cols, 128), low),
            pltpu.VMEM((CHUNKS, cols, 128), low),
            pltpu.VMEM((CHUNKS, cols, 128), wide),
            pltpu.VMEM((4, CHUNKS, cols, 128), low),
            pltpu.VMEM((2 * cols, chans), wide),
            dma,
            dma((2, HOPS, half)), dma((2, HOPS, half)), dma((2, HOPS, half)), dma((2, HOPS, half)),
            dma((CHUNKS, 2)), dma((CHUNKS, 2)), dma((CHUNKS,)), dma((CHUNKS,)),
            dma((CHUNKS,)), dma((CHUNKS,)), dma((CHUNKS, 2)), dma((CHUNKS, 2)),
        ],
        compiler_params=pltpu.CompilerParams(
            collective_id=0, has_side_effects=True, vmem_limit_bytes=52 << 20
        ),
    )(features, cotangent, depth_weight, point_weight, joining_weight, branch_mask)


def total_kernel(
    layout, piece, stored, scale, joining, point, depth, joining_out, point_out, depth_out,
    depth_rows, mine, from_x, from_y, from_z, gathered,
    x_send, x_recv, y_send, y_recv, z_send, z_recv, gy_send, gy_recv, gx_send, gx_recv,
):
    nx, nz, ny = layout
    strip = lax.axis_index("strip")
    branch = lax.axis_index("branch")
    y = lax.rem(strip, ny)
    z = lax.rem(strip // ny, nz)
    x = strip // (ny * nz)

    def x_peer(step):
        other = lax.rem(x + step, nx)
        return other, ((other * nz + z) * ny + y, branch)

    def y_peer(step):
        other = lax.rem(y + step, ny)
        return other, ((x * nz + z) * ny + other, branch)

    def z_peer(step):
        other = lax.rem(z + step, nz)
        return other, ((x * nz + other) * ny + y, branch)

    def remote(source, target, send_sem, recv_sem, device):
        return pltpu.make_async_remote_copy(
            src_ref=source, dst_ref=target, send_sem=send_sem, recv_sem=recv_sem,
            device_id=device, device_id_type=MESH,
        )

    barrier = pltpu.get_barrier_semaphore()
    greet(
        barrier,
        [x_peer(k)[1] for k in range(1, nx)]
        + [y_peer(k)[1] for k in range(1, ny)]
        + [z_peer(k)[1] for k in range(1, nz)],
    )

    depth_rows[...] = jnp.zeros_like(depth_rows)
    for tile in range(depth.shape[0]):
        for part in range(depth.shape[1]):
            depth_rows[part:part + 1, 128 * tile:128 * (tile + 1)] = jnp.sum(depth[tile, part], axis=0, keepdims=True)

    per_half = nx * ny // 2
    pieces = []
    for lane_half in range(2):
        tables = [
            (joining, joining_out, 0, 256, 128 * lane_half),
            (point, point_out, 256, 768, 128 * lane_half),
            (depth_rows, depth_out, 768, 784, 256 * lane_half),
            (depth_rows, depth_out, 784, 800, 256 * lane_half + 128),
        ]
        for index in range(per_half):
            at = lane_half * per_half + index
            start, stop = index * piece, (index + 1) * piece
            for source, target, first, last, lane in tables:
                low, high = max(start, first), min(stop, last)
                if low < high:
                    pieces.append((at // ny, at % ny, low - start, high - start, source, target, low - first, high - first, lane))
            if stop > 800:
                pieces.append((at // ny, at % ny, max(800 - start, 0), piece, None, None, 0, 0, 0))
    for px, py, low, high, source, _, first, last, lane in pieces:
        if source is None:
            mine[px, py, low:high, :] = jnp.zeros((high - low, 128), jnp.float32)
        else:
            mine[px, py, low:high, :] = source[first:last, lane:lane + 128]

    def x_copy(step):
        other, device = x_peer(step)
        return remote(mine.at[other], from_x.at[step - 1], x_send.at[step - 1], x_recv.at[step - 1], device)

    for step in range(1, nx):
        x_copy(step).start()
    for step in range(1, nx):
        x_copy(step).wait_recv()
    summed = mine[x]
    for step in range(1, nx):
        summed = summed + from_x[step - 1]
    from_y[0] = summed

    def y_copy(step):
        other, device = y_peer(step)
        return remote(from_y.at[0, other], from_y.at[1, step - 1], y_send.at[step - 1], y_recv.at[step - 1], device)

    for step in range(1, ny):
        y_copy(step).start()
    for step in range(1, ny):
        y_copy(step).wait_recv()
    summed = from_y[0, y]
    for step in range(1, ny):
        summed = summed + from_y[1, step - 1]
    from_z[z] = summed

    def z_copy(step):
        spot = from_z.at[z]
        return remote(spot, spot, z_send.at[step - 1], z_recv.at[step - 1], z_peer(step)[1])

    for step in range(1, nz):
        z_copy(step).start()
    for step in range(1, nz):
        z_copy(step).wait_recv()
    summed = from_z[0]
    for other in range(1, nz):
        summed = summed + from_z[other]
    gathered[x, y, 0:piece, :] = (summed * scale).astype(jnp.bfloat16)
    if stored > piece:
        gathered[x, y, piece:stored, :] = jnp.zeros((stored - piece, 128), jnp.bfloat16)

    def gy_copy(step):
        spot = gathered.at[x, y]
        return remote(spot, spot, gy_send.at[step - 1], gy_recv.at[step - 1], y_peer(step)[1])

    for step in range(1, ny):
        gy_copy(step).start()
    for step in range(1, ny):
        gy_copy(step).wait_recv()

    def gx_copy(step):
        spot = gathered.at[x]
        return remote(spot, spot, gx_send.at[step - 1], gx_recv.at[step - 1], x_peer(step)[1])

    for step in range(1, nx):
        gx_copy(step).start()
    for step in range(1, nx):
        gx_copy(step).wait_recv()

    for px, py, low, high, source, target, first, last, lane in pieces:
        if source is not None:
            target[first:last, lane:lane + 128] = gathered[px, py, 0:piece, :].astype(jnp.float32)[low:high, :]

    for step in range(1, nx):
        x_copy(step).wait_send()
        gx_copy(step).wait_send()
    for step in range(1, ny):
        y_copy(step).wait_send()
        gy_copy(step).wait_send()
    for step in range(1, nz):
        z_copy(step).wait_send()


def weight_totals(joining, point, depth, scale, strip_count):
    nx, nz, ny = strip_layout(strip_count)
    piece = -(-1600 // (nx * ny) // 8) * 8
    stored = -(-piece // 16) * 16
    vmem = pl.BlockSpec(memory_space=pltpu.VMEM)
    dma = pltpu.SemaphoreType.DMA
    depth_shape = (16, depth.shape[0] * 128)
    shapes = [joining.shape, point.shape, depth_shape]
    a, b, c = pl.pallas_call(
        functools.partial(total_kernel, (nx, nz, ny), piece, stored, scale),
        name="weight_totals",
        out_shape=tuple(jax.ShapeDtypeStruct(shape, jnp.float32) for shape in shapes),
        in_specs=[vmem] * 3,
        out_specs=(vmem,) * 3,
        scratch_shapes=[
            pltpu.VMEM(depth_shape, jnp.float32),
            pltpu.VMEM((nx, ny, piece, 128), jnp.float32),
            pltpu.VMEM((max(nx - 1, 1), ny, piece, 128), jnp.float32),
            pltpu.VMEM((2, ny, piece, 128), jnp.float32),
            pltpu.VMEM((nz, piece, 128), jnp.float32),
            pltpu.VMEM((nx, ny, stored, 128), jnp.bfloat16),
            dma((nx,)), dma((nx,)), dma((ny,)), dma((ny,)), dma((nz,)), dma((nz,)),
            dma((ny,)), dma((ny,)), dma((nx,)), dma((nx,)),
        ],
        compiler_params=pltpu.CompilerParams(
            collective_id=1, has_side_effects=True, vmem_limit_bytes=32 << 20
        ),
    )(joining, point, depth)
    return a, b, c[: depth.shape[1]]


def per_device(features, cotangent, depth_weight, point_weight, joining_weight, branch_mask):
    row_count, col_count, chan_count = features.shape
    strip_count = lax.axis_size("strip")
    pixel_scale = 1.0 / math.sqrt(row_count * col_count * strip_count)
    output, joining_part, point_part, depth_part = branch_step(
        features, cotangent, depth_weight, point_weight, joining_weight, branch_mask, strip_count
    )
    joining_total, point_total, depth_total = weight_totals(
        joining_part, point_part, depth_part, pixel_scale, strip_count
    )
    return (output, joining_total, point_total[None], depth_total[None])


def solution(mesh):
    placed = (
        P("strip", None, None),
        P("strip", None, "branch"),
        P("branch", None, None),
        P("branch", None, None),
        P("branch", None),
        P(),
    )
    return jax.shard_map(
        per_device,
        mesh=mesh,
        in_specs=placed,
        out_specs=(
            P("strip", None, "branch"),
            P("branch", None),
            P("branch", None, None),
            P("branch", None, None),
        ),
        check_vma=False,
    )
```

```python
import functools
import math

import jax
import jax.numpy as jnp
from jax import lax
from jax.experimental import pallas as pl
from jax.experimental.pallas import tpu as pltpu
from jax.sharding import PartitionSpec as P

DILATION_STEP = 6
HOPS = 3
MESH = pl.DeviceIdType.MESH

tanh_coef = 0.7978845608
cubic_coef = 0.044715
slope_coef = 0.134145


def contract_rows(left, right):
    return lax.dot_general(
        left, right, (((0,), (0,)), ((), ())), preferred_element_type=jnp.float32
    )


def contract_cols(left, right):
    return lax.dot_general(
        left, right, (((1,), (1,)), ((), ())), preferred_element_type=jnp.float32
    )


def greet(barrier, partners):
    for partner in partners:
        pl.semaphore_signal(barrier, inc=1, device_id=partner, device_id_type=MESH)
    pl.semaphore_wait(barrier, len(partners))


def strip_layout(strip_count):
    if strip_count == 128:
        return 4, 4, 8
    return {4: (2, 1, 2), 8: (2, 2, 2), 2: (2, 1, 1)}[strip_count]


CHUNKS = 4
LOW_ROWS = (2, 3, 0, 1)
HIGH_ROWS = (4, 5, 6, 7)
EDGE = 24


def swap_halves(low, high):
    lane = lax.broadcasted_iota(jnp.int32, low.shape, 1)
    left = lane < 64
    return (
        jnp.where(left, low, pltpu.roll(high, 64, 1)),
        jnp.where(left, pltpu.roll(low, 64, 1), high),
    )


def branch_kernel(
    strip_count, feat, cot, depth_w, point_w, join_w, mask, out, join_part, point_part, depth_part,
    ext, taps, dw_out, slope, branch_out, blocks, near, away, far, total, grads, grad_dw,
    own_sem, send, recv, pass_send, pass_recv,
    near_send, near_recv, far_send, far_recv, gfar_send, gfar_recv, gnear_send, gnear_recv,
):
    rows, cols, chans = feat.shape
    half = rows // 2
    tiles = chans // 128
    strip = lax.axis_index("strip")
    branch = lax.axis_index("branch")
    core = lax.rem(branch, 2)
    layer = branch // 2
    rate = (branch + 1) * DILATION_STEP
    beside = branch + 1 - 2 * core
    other = branch + 2 - 4 * layer
    beside_other = other + 1 - 2 * core
    sibling = (strip, beside)
    across = (strip, other)
    after = (lax.rem(strip + 1, strip_count), branch)
    before = (lax.rem(strip + strip_count - 1, strip_count), branch)
    active = mask[branch].astype(jnp.float32)
    greet(pltpu.get_barrier_semaphore(), [after, before, sibling, across])

    def remote(source, target, send_sem, recv_sem, device):
        return pltpu.make_async_remote_copy(
            src_ref=source, dst_ref=target, send_sem=send_sem, recv_sem=recv_sem,
            device_id=device, device_id_type=MESH,
        )

    centre = HOPS * rows

    def exists(offset):
        place = strip + offset
        return jnp.logical_and(place >= 0, place < strip_count)

    def line_row(line, side):
        return side * HIGH_ROWS[line] + (1 - side) * LOW_ROWS[line]

    def link_copy(way, step, line):
        at = 0 if way > 0 else 1
        row = line_row(line, core)
        if step == 0:
            source = feat.at[pl.ds(row, 1)]
        else:
            source = ext.at[pl.ds(centre - way * step * rows + row, 1)]
        return remote(
            source, ext.at[pl.ds(centre - way * (step + 1) * rows + row, 1)],
            send.at[at, step, line], recv.at[at, step, line], after if way > 0 else before,
        )

    def pass_copy(way, step, line, side):
        at = 0 if way > 0 else 1
        spot = ext.at[pl.ds(centre - way * (step + 1) * rows + line_row(line, side), 1)]
        return remote(spot, spot, pass_send.at[at, step, line], pass_recv.at[at, step, line], sibling)

    ways = (1, -1)

    def send_own(line):
        for way in ways:

            @pl.when(exists(way))
            def _():
                link_copy(way, 0, line).start()

    for line in range(half):
        send_own(line)
    own = pltpu.make_async_copy(feat, ext.at[pl.ds(centre, rows)], own_sem)
    own.start()

    for offset in range(1, HOPS + 1):
        for way in ways:

            @pl.when(jnp.logical_not(exists(offset * way)))
            def _():
                def fill(row, carry):
                    ext[centre + offset * way * rows + row] = jnp.zeros((cols, chans), ext.dtype)
                    return carry

                lax.fori_loop(0, rows, fill, 0)

    def clear(index, carry):
        for part in range(3):
            for tile in range(tiles):
                taps[index, part, tile, 0:EDGE, :] = jnp.zeros((EDGE, 128), jnp.float32)
                taps[index, part, tile, EDGE + cols:2 * EDGE + cols, :] = jnp.zeros((EDGE, 128), jnp.float32)
        return carry

    lax.fori_loop(0, rows, clear, 0)
    join_part[...] = jnp.zeros_like(join_part)
    point_part[...] = jnp.zeros_like(point_part)
    depth_part[...] = jnp.zeros_like(depth_part)

    def widen(row, part):
        at = centre + row + (part - 1) * rate
        for tile in range(tiles):
            taps[row, part, tile, EDGE:EDGE + cols, :] = ext[at, :, 128 * tile:128 * (tile + 1)].astype(jnp.float32)

    own.wait()

    def widen_own(row, carry):
        widen(row, 1)
        return carry

    lax.fori_loop(0, rows, widen_own, 0)

    def arrive(step, line):
        for way in ways:

            @pl.when(exists(-way * (step + 1)))
            def _():
                link_copy(way, step, line).wait_recv()

            if step + 1 < HOPS:

                @pl.when(jnp.logical_and(exists(-way * (step + 1)), exists(way)))
                def _():
                    link_copy(way, step + 1, line).start()

            @pl.when(exists(-way * (step + 1)))
            def _():
                pass_copy(way, step, line, core).start()

    def passed(step, line):
        for way in ways:

            @pl.when(exists(-way * (step + 1)))
            def _():
                pass_copy(way, step, line, 1 - core).wait_recv()

    def tap_columns(part):
        return pl.ds(EDGE + (part - 1) * rate, cols)

    def near_copy(chunk, side):
        return remote(
            blocks.at[2 * side + 1 - core, chunk], near.at[side, chunk],
            near_send.at[chunk, side], near_recv.at[chunk, side], sibling,
        )

    def far_copy(chunk):
        return remote(away.at[chunk], far.at[chunk], far_send.at[chunk], far_recv.at[chunk], across)

    def grad_far(chunk):
        spot = grads.at[branch, chunk]
        return remote(spot, spot, gfar_send.at[chunk], gfar_recv.at[chunk], across)

    def grad_near(chunk, which, block):
        spot = grads.at[block, chunk]
        return remote(spot, spot, gnear_send.at[chunk, which], gnear_recv.at[chunk, which], sibling)

    def forward(chunk):
        arrive(HOPS - 1, chunk)
        passed(HOPS - 1, chunk)
        for place, row in ((0, LOW_ROWS[chunk]), (1, HIGH_ROWS[chunk])):
            widen(row, 0)
            widen(row, 2)

            def depthwise(tile, carry):
                lanes = pl.ds(pl.multiple_of(tile * 128, 128), 128)
                weights = depth_w[0, :, lanes].astype(jnp.float32)
                summed = jnp.zeros((cols, 128), jnp.float32)
                for part in range(9):
                    piece = taps[row, part // 3, tile, tap_columns(part % 3), :]
                    summed = summed + piece * weights[part:part + 1, :]
                dw_out[chunk, place * cols:(place + 1) * cols, lanes] = summed.astype(jnp.bfloat16)
                return carry

            lax.fori_loop(0, tiles, depthwise, 0)
        pre = jnp.dot(dw_out[chunk], point_w[0], preferred_element_type=jnp.float32)
        inner = jnp.tanh(tanh_coef * (pre + cubic_coef * pre * pre * pre))
        slope[chunk] = 0.5 * (1.0 + inner) + 0.5 * pre * (1.0 - inner * inner) * tanh_coef * (
            1.0 + slope_coef * pre * pre
        )
        branch_out[chunk] = (0.5 * pre * (1.0 + inner) * active).astype(jnp.bfloat16)
        part_sum = jnp.dot(branch_out[chunk], join_w[...], preferred_element_type=jnp.float32)
        for pair in range(2):
            lanes = slice(128 * pair, 128 * (pair + 1))
            first, second = swap_halves(part_sum[:cols, lanes], part_sum[cols:, lanes])
            blocks[2 * pair, chunk] = first.astype(jnp.bfloat16)
            blocks[2 * pair + 1, chunk] = second.astype(jnp.bfloat16)
        for side in range(2):
            near_copy(chunk, side).start()

    def pair_sum(chunk):
        for side in range(2):
            near_copy(chunk, side).wait_recv()
        there = 1 - layer
        away[chunk] = (
            blocks[2 * there + core, chunk].astype(jnp.float32) + near[there, chunk].astype(jnp.float32)
        ).astype(jnp.bfloat16)
        far_copy(chunk).start()
        total[chunk] = blocks[branch, chunk].astype(jnp.float32) + near[layer, chunk].astype(jnp.float32)

    def finish_sum(chunk):
        far_copy(chunk).wait_recv()
        joined = total[chunk] + far[chunk].astype(jnp.float32)
        inner = jnp.tanh(tanh_coef * (joined + cubic_coef * joined * joined * joined))
        rise = 0.5 * (1.0 + inner) + 0.5 * joined * (1.0 - inner * inner) * tanh_coef * (
            1.0 + slope_coef * joined * joined
        )
        low_row, high_row = LOW_ROWS[chunk], HIGH_ROWS[chunk]
        given = jnp.concatenate([cot[low_row].astype(jnp.float32), cot[high_row].astype(jnp.float32)], axis=1)
        grads[branch, chunk] = (given * rise).astype(jnp.bfloat16)
        grad_far(chunk).start()
        grad_near(chunk, 0, branch).start()
        result = (0.5 * joined * (1.0 + inner)).astype(out.dtype)
        out[low_row] = result[:, :64]
        out[high_row] = result[:, 64:]

    def hand_on(chunk):
        grad_far(chunk).wait_recv()
        grad_near(chunk, 1, other).start()

    def backward(chunk):
        grad_near(chunk, 0, beside).wait_recv()
        grad_near(chunk, 1, beside_other).wait_recv()
        low_parts, high_parts = [], []
        for pair in range(2):
            low, high = swap_halves(
                grads[2 * pair, chunk].astype(jnp.float32), grads[2 * pair + 1, chunk].astype(jnp.float32)
            )
            low_parts.append(low)
            high_parts.append(high)
        full_grad = jnp.concatenate(
            [jnp.concatenate(low_parts, axis=1), jnp.concatenate(high_parts, axis=1)], axis=0
        ).astype(jnp.bfloat16)
        grad_branch = contract_cols(full_grad, join_w[...]) * active
        grad_pre = (grad_branch * slope[chunk]).astype(jnp.bfloat16)
        grad_dw[...] = contract_cols(grad_pre, point_w[0])
        join_part[...] += contract_rows(branch_out[chunk], full_grad)
        point_part[...] += contract_rows(dw_out[chunk], grad_pre)
        for place, row in ((0, LOW_ROWS[chunk]), (1, HIGH_ROWS[chunk])):

            def depth_sums(tile, carry):
                here = grad_dw[place * cols:(place + 1) * cols, pl.ds(pl.multiple_of(tile * 128, 128), 128)]
                for part in range(9):
                    product = here * taps[row, part // 3, tile, tap_columns(part % 3), :]
                    depth_part[tile, part] += jnp.sum(product.reshape(cols // 8, 8, 128), axis=0)
                return carry

            lax.fori_loop(0, tiles, depth_sums, 0)

    for step in range(HOPS - 1):
        for line in range(half):
            arrive(step, line)
    for step in range(HOPS - 1):
        for line in range(half):
            passed(step, line)

    stages = (forward, pair_sum, finish_sum, hand_on, backward)
    for turn in range(CHUNKS + len(stages) - 1):
        for index, stage in enumerate(stages):
            if 0 <= turn - index < CHUNKS:
                stage(turn - index)

    for step in range(HOPS):
        for line in range(half):
            for way in ways:

                @pl.when(jnp.logical_and(exists(-way * step), exists(way)))
                def _():
                    link_copy(way, step, line).wait_send()

                @pl.when(exists(-way * (step + 1)))
                def _():
                    pass_copy(way, step, line, core).wait_send()

    for chunk in range(CHUNKS):
        for side in range(2):
            near_copy(chunk, side).wait_send()
        far_copy(chunk).wait_send()
        grad_far(chunk).wait_send()
        grad_near(chunk, 0, branch).wait_send()
        grad_near(chunk, 1, other).wait_send()


def branch_step(features, cotangent, depth_weight, point_weight, joining_weight, branch_mask, strip_count):
    rows, cols, chans = features.shape
    width = point_weight.shape[2]
    half = rows // 2
    tiles = chans // 128
    vmem = pl.BlockSpec(memory_space=pltpu.VMEM)
    dma = pltpu.SemaphoreType.DMA
    low, wide = jnp.bfloat16, jnp.float32
    return pl.pallas_call(
        functools.partial(branch_kernel, strip_count),
        name="branch_step",
        out_shape=(
            jax.ShapeDtypeStruct(cotangent.shape, low),
            jax.ShapeDtypeStruct((width, width), wide),
            jax.ShapeDtypeStruct((chans, width), wide),
            jax.ShapeDtypeStruct((tiles, 9, 8, 128), wide),
        ),
        in_specs=[pl.BlockSpec(memory_space=pl.ANY)] + [vmem] * 4 + [pl.BlockSpec(memory_space=pltpu.SMEM)],
        out_specs=(vmem,) * 4,
        scratch_shapes=[
            pltpu.VMEM(((2 * HOPS + 1) * rows, cols, chans), low),
            pltpu.VMEM((rows, 3, tiles, cols + 2 * EDGE, 128), wide),
            pltpu.VMEM((CHUNKS, 2 * cols, chans), low),
            pltpu.VMEM((CHUNKS, 2 * cols, width), wide),
            pltpu.VMEM((CHUNKS, 2 * cols, width), low),
            pltpu.VMEM((4, CHUNKS, cols, 128), low),
            pltpu.VMEM((2, CHUNKS, cols, 128), low),
            pltpu.VMEM((CHUNKS, cols, 128), low),
            pltpu.VMEM((CHUNKS, cols, 128), low),
            pltpu.VMEM((CHUNKS, cols, 128), wide),
            pltpu.VMEM((4, CHUNKS, cols, 128), low),
            pltpu.VMEM((2 * cols, chans), wide),
            dma,
            dma((2, HOPS, half)), dma((2, HOPS, half)), dma((2, HOPS, half)), dma((2, HOPS, half)),
            dma((CHUNKS, 2)), dma((CHUNKS, 2)), dma((CHUNKS,)), dma((CHUNKS,)),
            dma((CHUNKS,)), dma((CHUNKS,)), dma((CHUNKS, 2)), dma((CHUNKS, 2)),
        ],
        compiler_params=pltpu.CompilerParams(
            collective_id=0, has_side_effects=True, vmem_limit_bytes=52 << 20
        ),
    )(features, cotangent, depth_weight, point_weight, joining_weight, branch_mask)


def total_kernel(
    layout, piece, stored, scale, joining, point, depth, joining_out, point_out, depth_out,
    depth_rows, mine, sent, from_x, from_y, from_z, gathered,
    x_send, x_recv, y_send, y_recv, z_send, z_recv, gy_send, gy_recv, gx_send, gx_recv,
):
    nx, nz, ny = layout
    strip = lax.axis_index("strip")
    branch = lax.axis_index("branch")
    y = lax.rem(strip, ny)
    z = lax.rem(strip // ny, nz)
    x = strip // (ny * nz)

    def x_peer(step):
        other = lax.rem(x + step, nx)
        return other, ((other * nz + z) * ny + y, branch)

    def y_peer(step):
        other = lax.rem(y + step, ny)
        return other, ((x * nz + z) * ny + other, branch)

    def z_peer(step):
        other = lax.rem(z + step, nz)
        return other, ((x * nz + other) * ny + y, branch)

    def remote(source, target, send_sem, recv_sem, device):
        return pltpu.make_async_remote_copy(
            src_ref=source, dst_ref=target, send_sem=send_sem, recv_sem=recv_sem,
            device_id=device, device_id_type=MESH,
        )

    barrier = pltpu.get_barrier_semaphore()
    greet(
        barrier,
        [x_peer(k)[1] for k in range(1, nx)]
        + [y_peer(k)[1] for k in range(1, ny)]
        + [z_peer(k)[1] for k in range(1, nz)],
    )

    depth_rows[...] = jnp.zeros_like(depth_rows)
    for tile in range(depth.shape[0]):
        for part in range(depth.shape[1]):
            depth_rows[part:part + 1, 128 * tile:128 * (tile + 1)] = jnp.sum(depth[tile, part], axis=0, keepdims=True)

    per_half = nx * ny // 2
    pieces = []
    for lane_half in range(2):
        tables = [
            (joining, joining_out, 0, 256, 128 * lane_half),
            (point, point_out, 256, 768, 128 * lane_half),
            (depth_rows, depth_out, 768, 784, 256 * lane_half),
            (depth_rows, depth_out, 784, 800, 256 * lane_half + 128),
        ]
        for index in range(per_half):
            at = lane_half * per_half + index
            start, stop = index * piece, (index + 1) * piece
            for source, target, first, last, lane in tables:
                low, high = max(start, first), min(stop, last)
                if low < high:
                    pieces.append((at // ny, at % ny, low - start, high - start, source, target, low - first, high - first, lane))
            if stop > 800:
                pieces.append((at // ny, at % ny, max(800 - start, 0), piece, None, None, 0, 0, 0))
    for px, py, low, high, source, _, first, last, lane in pieces:
        if source is None:
            mine[px, py, low:high, :] = jnp.zeros((high - low, 128), jnp.float32)
        else:
            mine[px, py, low:high, :] = source[first:last, lane:lane + 128]

    for px in range(nx):
        for py in range(ny):
            sent[px, py, 0:piece, :] = mine[px, py].astype(jnp.bfloat16)
            if stored > piece:
                sent[px, py, piece:stored, :] = jnp.zeros((stored - piece, 128), jnp.bfloat16)

    def x_copy(step):
        other, device = x_peer(step)
        return remote(sent.at[other], from_x.at[step - 1], x_send.at[step - 1], x_recv.at[step - 1], device)

    for step in range(1, nx):
        x_copy(step).start()
    for step in range(1, nx):
        x_copy(step).wait_recv()
    summed = mine[x]
    for step in range(1, nx):
        summed = summed + from_x[step - 1].astype(jnp.float32)[:, 0:piece, :]
    mine[0] = summed
    for py in range(ny):
        from_y[0, py, 0:piece, :] = mine[0, py].astype(jnp.bfloat16)
        if stored > piece:
            from_y[0, py, piece:stored, :] = jnp.zeros((stored - piece, 128), jnp.bfloat16)

    def y_copy(step):
        other, device = y_peer(step)
        return remote(from_y.at[0, other], from_y.at[1, step - 1], y_send.at[step - 1], y_recv.at[step - 1], device)

    for step in range(1, ny):
        y_copy(step).start()
    for step in range(1, ny):
        y_copy(step).wait_recv()
    summed = mine[0, y]
    for step in range(1, ny):
        summed = summed + from_y[1, step - 1].astype(jnp.float32)[0:piece, :]
    from_z[z] = summed

    def z_copy(step):
        spot = from_z.at[z]
        return remote(spot, spot, z_send.at[step - 1], z_recv.at[step - 1], z_peer(step)[1])

    for step in range(1, nz):
        z_copy(step).start()
    for step in range(1, nz):
        z_copy(step).wait_recv()
    summed = from_z[0]
    for other in range(1, nz):
        summed = summed + from_z[other]
    gathered[x, y, 0:piece, :] = (summed * scale).astype(jnp.bfloat16)
    if stored > piece:
        gathered[x, y, piece:stored, :] = jnp.zeros((stored - piece, 128), jnp.bfloat16)

    def gy_copy(step):
        spot = gathered.at[x, y]
        return remote(spot, spot, gy_send.at[step - 1], gy_recv.at[step - 1], y_peer(step)[1])

    for step in range(1, ny):
        gy_copy(step).start()
    for step in range(1, ny):
        gy_copy(step).wait_recv()

    def gx_copy(step):
        spot = gathered.at[x]
        return remote(spot, spot, gx_send.at[step - 1], gx_recv.at[step - 1], x_peer(step)[1])

    for step in range(1, nx):
        gx_copy(step).start()
    for step in range(1, nx):
        gx_copy(step).wait_recv()

    for px, py, low, high, source, target, first, last, lane in pieces:
        if source is not None:
            target[first:last, lane:lane + 128] = gathered[px, py, 0:piece, :].astype(jnp.float32)[low:high, :]

    for step in range(1, nx):
        x_copy(step).wait_send()
        gx_copy(step).wait_send()
    for step in range(1, ny):
        y_copy(step).wait_send()
        gy_copy(step).wait_send()
    for step in range(1, nz):
        z_copy(step).wait_send()


def weight_totals(joining, point, depth, scale, strip_count):
    nx, nz, ny = strip_layout(strip_count)
    piece = -(-1600 // (nx * ny) // 8) * 8
    stored = -(-piece // 16) * 16
    vmem = pl.BlockSpec(memory_space=pltpu.VMEM)
    dma = pltpu.SemaphoreType.DMA
    depth_shape = (16, depth.shape[0] * 128)
    shapes = [joining.shape, point.shape, depth_shape]
    a, b, c = pl.pallas_call(
        functools.partial(total_kernel, (nx, nz, ny), piece, stored, scale),
        name="weight_totals",
        out_shape=tuple(jax.ShapeDtypeStruct(shape, jnp.float32) for shape in shapes),
        in_specs=[vmem] * 3,
        out_specs=(vmem,) * 3,
        scratch_shapes=[
            pltpu.VMEM(depth_shape, jnp.float32),
            pltpu.VMEM((nx, ny, piece, 128), jnp.float32),
            pltpu.VMEM((nx, ny, stored, 128), jnp.bfloat16),
            pltpu.VMEM((max(nx - 1, 1), ny, stored, 128), jnp.bfloat16),
            pltpu.VMEM((2, ny, stored, 128), jnp.bfloat16),
            pltpu.VMEM((nz, piece, 128), jnp.float32),
            pltpu.VMEM((nx, ny, stored, 128), jnp.bfloat16),
            dma((nx,)), dma((nx,)), dma((ny,)), dma((ny,)), dma((nz,)), dma((nz,)),
            dma((ny,)), dma((ny,)), dma((nx,)), dma((nx,)),
        ],
        compiler_params=pltpu.CompilerParams(
            collective_id=1, has_side_effects=True, vmem_limit_bytes=32 << 20
        ),
    )(joining, point, depth)
    return a, b, c[: depth.shape[1]]


def per_device(features, cotangent, depth_weight, point_weight, joining_weight, branch_mask):
    row_count, col_count, chan_count = features.shape
    strip_count = lax.axis_size("strip")
    pixel_scale = 1.0 / math.sqrt(row_count * col_count * strip_count)
    output, joining_part, point_part, depth_part = branch_step(
        features, cotangent, depth_weight, point_weight, joining_weight, branch_mask, strip_count
    )
    joining_total, point_total, depth_total = weight_totals(
        joining_part, point_part, depth_part, pixel_scale, strip_count
    )
    return (output, joining_total, point_total[None], depth_total[None])


def solution(mesh):
    placed = (
        P("strip", None, None),
        P("strip", None, "branch"),
        P("branch", None, None),
        P("branch", None, None),
        P("branch", None),
        P(),
    )
    return jax.shard_map(
        per_device,
        mesh=mesh,
        in_specs=placed,
        out_specs=(
            P("strip", None, "branch"),
            P("branch", None),
            P("branch", None, None),
            P("branch", None, None),
        ),
        check_vma=False,
    )
```

```python
import functools
import math

import jax
import jax.numpy as jnp
from jax import lax
from jax.experimental import pallas as pl
from jax.experimental.pallas import tpu as pltpu
from jax.sharding import PartitionSpec as P

DILATION_STEP = 6
HOPS = 3
MESH = pl.DeviceIdType.MESH

tanh_coef = 0.7978845608
cubic_coef = 0.044715
slope_coef = 0.134145


def contract_rows(left, right):
    return lax.dot_general(
        left, right, (((0,), (0,)), ((), ())), preferred_element_type=jnp.float32
    )


def contract_cols(left, right):
    return lax.dot_general(
        left, right, (((1,), (1,)), ((), ())), preferred_element_type=jnp.float32
    )


def greet(barrier, partners):
    for partner in partners:
        pl.semaphore_signal(barrier, inc=1, device_id=partner, device_id_type=MESH)
    pl.semaphore_wait(barrier, len(partners))


def strip_layout(strip_count):
    if strip_count == 128:
        return 4, 4, 8
    return {4: (2, 1, 2), 8: (2, 2, 2), 2: (2, 1, 1)}[strip_count]


CHUNKS = 4
LOW_ROWS = (2, 3, 0, 1)
HIGH_ROWS = (4, 5, 6, 7)
EDGE = 24


def swap_halves(low, high):
    lane = lax.broadcasted_iota(jnp.int32, low.shape, 1)
    left = lane < 64
    return (
        jnp.where(left, low, pltpu.roll(high, 64, 1)),
        jnp.where(left, pltpu.roll(low, 64, 1), high),
    )


def branch_kernel(
    strip_count, feat, cot, depth_w, point_w, join_w, mask, out, join_part, point_part, depth_part,
    ext, taps, dw_out, slope, branch_out, blocks, near, away, far, total, grads, grad_dw,
    own_sem, send, recv, pass_send, pass_recv,
    near_send, near_recv, far_send, far_recv, gfar_send, gfar_recv, gnear_send, gnear_recv,
):
    rows, cols, chans = feat.shape
    half = rows // 2
    tiles = chans // 128
    strip = lax.axis_index("strip")
    branch = lax.axis_index("branch")
    core = lax.rem(branch, 2)
    layer = branch // 2
    rate = (branch + 1) * DILATION_STEP
    beside = branch + 1 - 2 * core
    other = branch + 2 - 4 * layer
    beside_other = other + 1 - 2 * core
    sibling = (strip, beside)
    across = (strip, other)
    after = (lax.rem(strip + 1, strip_count), branch)
    before = (lax.rem(strip + strip_count - 1, strip_count), branch)
    active = mask[branch].astype(jnp.float32)
    greet(pltpu.get_barrier_semaphore(), [after, before, sibling, across])

    def remote(source, target, send_sem, recv_sem, device):
        return pltpu.make_async_remote_copy(
            src_ref=source, dst_ref=target, send_sem=send_sem, recv_sem=recv_sem,
            device_id=device, device_id_type=MESH,
        )

    centre = HOPS * rows

    def exists(offset):
        place = strip + offset
        return jnp.logical_and(place >= 0, place < strip_count)

    def line_row(line, side):
        return side * HIGH_ROWS[line] + (1 - side) * LOW_ROWS[line]

    def link_copy(way, step, line):
        at = 0 if way > 0 else 1
        row = line_row(line, core)
        if step == 0:
            source = feat.at[pl.ds(row, 1)]
        else:
            source = ext.at[pl.ds(centre - way * step * rows + row, 1)]
        return remote(
            source, ext.at[pl.ds(centre - way * (step + 1) * rows + row, 1)],
            send.at[at, step, line], recv.at[at, step, line], after if way > 0 else before,
        )

    def pass_copy(way, step, line, side):
        at = 0 if way > 0 else 1
        spot = ext.at[pl.ds(centre - way * (step + 1) * rows + line_row(line, side), 1)]
        return remote(spot, spot, pass_send.at[at, step, line], pass_recv.at[at, step, line], sibling)

    ways = (1, -1)

    def send_own(line):
        for way in ways:

            @pl.when(exists(way))
            def _():
                link_copy(way, 0, line).start()

    for line in range(half):
        send_own(line)
    own = pltpu.make_async_copy(feat, ext.at[pl.ds(centre, rows)], own_sem)
    own.start()

    for offset in range(1, HOPS + 1):
        for way in ways:

            @pl.when(jnp.logical_not(exists(offset * way)))
            def _():
                def fill(row, carry):
                    ext[centre + offset * way * rows + row] = jnp.zeros((cols, chans), ext.dtype)
                    return carry

                lax.fori_loop(0, rows, fill, 0)

    def clear(index, carry):
        for part in range(3):
            for tile in range(tiles):
                taps[index, part, tile, 0:EDGE, :] = jnp.zeros((EDGE, 128), jnp.float32)
                taps[index, part, tile, EDGE + cols:2 * EDGE + cols, :] = jnp.zeros((EDGE, 128), jnp.float32)
        return carry

    lax.fori_loop(0, rows, clear, 0)
    join_part[...] = jnp.zeros_like(join_part)
    point_part[...] = jnp.zeros_like(point_part)
    depth_part[...] = jnp.zeros_like(depth_part)

    def widen(row, part):
        at = centre + row + (part - 1) * rate
        for tile in range(tiles):
            taps[row, part, tile, EDGE:EDGE + cols, :] = ext[at, :, 128 * tile:128 * (tile + 1)].astype(jnp.float32)

    own.wait()

    def widen_own(row, carry):
        widen(row, 1)
        return carry

    lax.fori_loop(0, rows, widen_own, 0)

    def arrive(step, line):
        for way in ways:

            @pl.when(exists(-way * (step + 1)))
            def _():
                link_copy(way, step, line).wait_recv()

            if step + 1 < HOPS:

                @pl.when(jnp.logical_and(exists(-way * (step + 1)), exists(way)))
                def _():
                    link_copy(way, step + 1, line).start()

            @pl.when(exists(-way * (step + 1)))
            def _():
                pass_copy(way, step, line, core).start()

    def passed(step, line):
        for way in ways:

            @pl.when(exists(-way * (step + 1)))
            def _():
                pass_copy(way, step, line, 1 - core).wait_recv()

    def tap_columns(part):
        return pl.ds(EDGE + (part - 1) * rate, cols)

    def near_copy(chunk, side):
        return remote(
            blocks.at[2 * side + 1 - core, chunk], near.at[side, chunk],
            near_send.at[chunk, side], near_recv.at[chunk, side], sibling,
        )

    def far_copy(chunk):
        return remote(away.at[chunk], far.at[chunk], far_send.at[chunk], far_recv.at[chunk], across)

    def grad_far(chunk):
        spot = grads.at[branch, chunk]
        return remote(spot, spot, gfar_send.at[chunk], gfar_recv.at[chunk], across)

    def grad_near(chunk, which, block):
        spot = grads.at[block, chunk]
        return remote(spot, spot, gnear_send.at[chunk, which], gnear_recv.at[chunk, which], sibling)

    def forward(chunk):
        arrive(HOPS - 1, chunk)
        passed(HOPS - 1, chunk)
        for place, row in ((0, LOW_ROWS[chunk]), (1, HIGH_ROWS[chunk])):
            widen(row, 0)
            widen(row, 2)

            def depthwise(tile, carry):
                lanes = pl.ds(pl.multiple_of(tile * 128, 128), 128)
                weights = depth_w[0, :, lanes].astype(jnp.float32)
                summed = jnp.zeros((cols, 128), jnp.float32)
                for part in range(9):
                    piece = taps[row, part // 3, tile, tap_columns(part % 3), :]
                    summed = summed + piece * weights[part:part + 1, :]
                dw_out[chunk, place * cols:(place + 1) * cols, lanes] = summed.astype(jnp.bfloat16)
                return carry

            lax.fori_loop(0, tiles, depthwise, 0)
        pre = jnp.dot(dw_out[chunk], point_w[0], preferred_element_type=jnp.float32)
        inner = jnp.tanh(tanh_coef * (pre + cubic_coef * pre * pre * pre))
        slope[chunk] = 0.5 * (1.0 + inner) + 0.5 * pre * (1.0 - inner * inner) * tanh_coef * (
            1.0 + slope_coef * pre * pre
        )
        branch_out[chunk] = (0.5 * pre * (1.0 + inner) * active).astype(jnp.bfloat16)
        part_sum = jnp.dot(branch_out[chunk], join_w[...], preferred_element_type=jnp.float32)
        for pair in range(2):
            lanes = slice(128 * pair, 128 * (pair + 1))
            first, second = swap_halves(part_sum[:cols, lanes], part_sum[cols:, lanes])
            blocks[2 * pair, chunk] = first.astype(jnp.bfloat16)
            blocks[2 * pair + 1, chunk] = second.astype(jnp.bfloat16)
        for side in range(2):
            near_copy(chunk, side).start()

    def pair_sum(chunk):
        for side in range(2):
            near_copy(chunk, side).wait_recv()
        there = 1 - layer
        away[chunk] = (
            blocks[2 * there + core, chunk].astype(jnp.float32) + near[there, chunk].astype(jnp.float32)
        ).astype(jnp.bfloat16)
        far_copy(chunk).start()
        total[chunk] = blocks[branch, chunk].astype(jnp.float32) + near[layer, chunk].astype(jnp.float32)

    def finish_sum(chunk):
        far_copy(chunk).wait_recv()
        joined = total[chunk] + far[chunk].astype(jnp.float32)
        inner = jnp.tanh(tanh_coef * (joined + cubic_coef * joined * joined * joined))
        rise = 0.5 * (1.0 + inner) + 0.5 * joined * (1.0 - inner * inner) * tanh_coef * (
            1.0 + slope_coef * joined * joined
        )
        low_row, high_row = LOW_ROWS[chunk], HIGH_ROWS[chunk]
        given = jnp.concatenate([cot[low_row].astype(jnp.float32), cot[high_row].astype(jnp.float32)], axis=1)
        grads[branch, chunk] = (given * rise).astype(jnp.bfloat16)
        grad_far(chunk).start()
        grad_near(chunk, 0, branch).start()
        result = (0.5 * joined * (1.0 + inner)).astype(out.dtype)
        out[low_row] = result[:, :64]
        out[high_row] = result[:, 64:]

    def hand_on(chunk):
        grad_far(chunk).wait_recv()
        grad_near(chunk, 1, other).start()

    def backward(chunk):
        grad_near(chunk, 0, beside).wait_recv()
        grad_near(chunk, 1, beside_other).wait_recv()
        low_parts, high_parts = [], []
        for pair in range(2):
            low, high = swap_halves(
                grads[2 * pair, chunk].astype(jnp.float32), grads[2 * pair + 1, chunk].astype(jnp.float32)
            )
            low_parts.append(low)
            high_parts.append(high)
        full_grad = jnp.concatenate(
            [jnp.concatenate(low_parts, axis=1), jnp.concatenate(high_parts, axis=1)], axis=0
        ).astype(jnp.bfloat16)
        grad_branch = contract_cols(full_grad, join_w[...]) * active
        grad_pre = (grad_branch * slope[chunk]).astype(jnp.bfloat16)
        grad_dw[...] = contract_cols(grad_pre, point_w[0])
        join_part[...] += contract_rows(branch_out[chunk], full_grad)
        point_part[...] += contract_rows(dw_out[chunk], grad_pre)
        for place, row in ((0, LOW_ROWS[chunk]), (1, HIGH_ROWS[chunk])):

            def depth_sums(tile, carry):
                here = grad_dw[place * cols:(place + 1) * cols, pl.ds(pl.multiple_of(tile * 128, 128), 128)]
                for part in range(9):
                    product = here * taps[row, part // 3, tile, tap_columns(part % 3), :]
                    depth_part[tile, part] += jnp.sum(product.reshape(cols // 8, 8, 128), axis=0)
                return carry

            lax.fori_loop(0, tiles, depth_sums, 0)

    for step in range(HOPS - 1):
        for line in range(half):
            arrive(step, line)
    for step in range(HOPS - 1):
        for line in range(half):
            passed(step, line)

    stages = (forward, pair_sum, finish_sum, hand_on, backward)
    for turn in range(CHUNKS + len(stages) - 1):
        for index, stage in enumerate(stages):
            if 0 <= turn - index < CHUNKS:
                stage(turn - index)

    for step in range(HOPS):
        for line in range(half):
            for way in ways:

                @pl.when(jnp.logical_and(exists(-way * step), exists(way)))
                def _():
                    link_copy(way, step, line).wait_send()

                @pl.when(exists(-way * (step + 1)))
                def _():
                    pass_copy(way, step, line, core).wait_send()

    for chunk in range(CHUNKS):
        for side in range(2):
            near_copy(chunk, side).wait_send()
        far_copy(chunk).wait_send()
        grad_far(chunk).wait_send()
        grad_near(chunk, 0, branch).wait_send()
        grad_near(chunk, 1, other).wait_send()


def branch_step(features, cotangent, depth_weight, point_weight, joining_weight, branch_mask, strip_count):
    rows, cols, chans = features.shape
    width = point_weight.shape[2]
    half = rows // 2
    tiles = chans // 128
    vmem = pl.BlockSpec(memory_space=pltpu.VMEM)
    dma = pltpu.SemaphoreType.DMA
    low, wide = jnp.bfloat16, jnp.float32
    return pl.pallas_call(
        functools.partial(branch_kernel, strip_count),
        name="branch_step",
        out_shape=(
            jax.ShapeDtypeStruct(cotangent.shape, low),
            jax.ShapeDtypeStruct((width, width), wide),
            jax.ShapeDtypeStruct((chans, width), wide),
            jax.ShapeDtypeStruct((tiles, 9, 8, 128), wide),
        ),
        in_specs=[pl.BlockSpec(memory_space=pl.ANY)] + [vmem] * 4 + [pl.BlockSpec(memory_space=pltpu.SMEM)],
        out_specs=(vmem,) * 4,
        scratch_shapes=[
            pltpu.VMEM(((2 * HOPS + 1) * rows, cols, chans), low),
            pltpu.VMEM((rows, 3, tiles, cols + 2 * EDGE, 128), wide),
            pltpu.VMEM((CHUNKS, 2 * cols, chans), low),
            pltpu.VMEM((CHUNKS, 2 * cols, width), wide),
            pltpu.VMEM((CHUNKS, 2 * cols, width), low),
            pltpu.VMEM((4, CHUNKS, cols, 128), low),
            pltpu.VMEM((2, CHUNKS, cols, 128), low),
            pltpu.VMEM((CHUNKS, cols, 128), low),
            pltpu.VMEM((CHUNKS, cols, 128), low),
            pltpu.VMEM((CHUNKS, cols, 128), wide),
            pltpu.VMEM((4, CHUNKS, cols, 128), low),
            pltpu.VMEM((2 * cols, chans), wide),
            dma,
            dma((2, HOPS, half)), dma((2, HOPS, half)), dma((2, HOPS, half)), dma((2, HOPS, half)),
            dma((CHUNKS, 2)), dma((CHUNKS, 2)), dma((CHUNKS,)), dma((CHUNKS,)),
            dma((CHUNKS,)), dma((CHUNKS,)), dma((CHUNKS, 2)), dma((CHUNKS, 2)),
        ],
        compiler_params=pltpu.CompilerParams(
            collective_id=0, has_side_effects=True, vmem_limit_bytes=52 << 20
        ),
    )(features, cotangent, depth_weight, point_weight, joining_weight, branch_mask)


def total_kernel(
    layout, piece, stored, scale, joining, point, depth, joining_out, point_out, depth_out,
    depth_rows, mine, sent, from_x, from_y, from_z, gathered,
    x_send, x_recv, y_send, y_recv, z_send, z_recv, gy_send, gy_recv, gx_send, gx_recv,
):
    nx, nz, ny = layout
    strip = lax.axis_index("strip")
    branch = lax.axis_index("branch")
    y = lax.rem(strip, ny)
    z = lax.rem(strip // ny, nz)
    x = strip // (ny * nz)

    def x_peer(step):
        other = lax.rem(x + step, nx)
        return other, ((other * nz + z) * ny + y, branch)

    def y_peer(step):
        other = lax.rem(y + step, ny)
        return other, ((x * nz + z) * ny + other, branch)

    def z_peer(step):
        other = lax.rem(z + step, nz)
        return other, ((x * nz + other) * ny + y, branch)

    def remote(source, target, send_sem, recv_sem, device):
        return pltpu.make_async_remote_copy(
            src_ref=source, dst_ref=target, send_sem=send_sem, recv_sem=recv_sem,
            device_id=device, device_id_type=MESH,
        )

    barrier = pltpu.get_barrier_semaphore()
    greet(
        barrier,
        [x_peer(k)[1] for k in range(1, nx)]
        + [y_peer(k)[1] for k in range(1, ny)]
        + [z_peer(k)[1] for k in range(1, nz)],
    )

    depth_rows[...] = jnp.zeros_like(depth_rows)
    for tile in range(depth.shape[0]):
        for part in range(depth.shape[1]):
            depth_rows[part:part + 1, 128 * tile:128 * (tile + 1)] = jnp.sum(depth[tile, part], axis=0, keepdims=True)

    per_half = nx * ny // 2
    pieces = []
    for lane_half in range(2):
        tables = [
            (joining, joining_out, 0, 256, 128 * lane_half),
            (point, point_out, 256, 768, 128 * lane_half),
            (depth_rows, depth_out, 768, 784, 256 * lane_half),
            (depth_rows, depth_out, 784, 800, 256 * lane_half + 128),
        ]
        for index in range(per_half):
            at = lane_half * per_half + index
            start, stop = index * piece, (index + 1) * piece
            for source, target, first, last, lane in tables:
                low, high = max(start, first), min(stop, last)
                if low < high:
                    pieces.append((at // ny, at % ny, low - start, high - start, source, target, low - first, high - first, lane))
            if stop > 800:
                pieces.append((at // ny, at % ny, max(800 - start, 0), piece, None, None, 0, 0, 0))
    for px, py, low, high, source, _, first, last, lane in pieces:
        if source is None:
            mine[px, py, low:high, :] = jnp.zeros((high - low, 128), jnp.float32)
        else:
            mine[px, py, low:high, :] = source[first:last, lane:lane + 128]

    def x_copy(step):
        other, device = x_peer(step)
        return remote(sent.at[other], from_x.at[step - 1], x_send.at[step - 1], x_recv.at[step - 1], device)

    for step in range(1, nx):
        px = x_peer(step)[0]
        for py in range(ny):
            sent[px, py, 0:piece, :] = mine[px, py].astype(jnp.bfloat16)
            if stored > piece:
                sent[px, py, piece:stored, :] = jnp.zeros((stored - piece, 128), jnp.bfloat16)
        x_copy(step).start()
    for step in range(1, nx):
        x_copy(step).wait_recv()
    summed = mine[x]
    for step in range(1, nx):
        summed = summed + from_x[step - 1].astype(jnp.float32)[:, 0:piece, :]
    mine[0] = summed
    for py in range(ny):
        from_y[0, py, 0:piece, :] = mine[0, py].astype(jnp.bfloat16)
        if stored > piece:
            from_y[0, py, piece:stored, :] = jnp.zeros((stored - piece, 128), jnp.bfloat16)

    def y_copy(step):
        other, device = y_peer(step)
        return remote(from_y.at[0, other], from_y.at[1, step - 1], y_send.at[step - 1], y_recv.at[step - 1], device)

    for step in range(1, ny):
        y_copy(step).start()
    for step in range(1, ny):
        y_copy(step).wait_recv()
    summed = mine[0, y]
    for step in range(1, ny):
        summed = summed + from_y[1, step - 1].astype(jnp.float32)[0:piece, :]
    from_z[z, 0:piece, :] = summed.astype(jnp.bfloat16)
    if stored > piece:
        from_z[z, piece:stored, :] = jnp.zeros((stored - piece, 128), jnp.bfloat16)

    def z_copy(step):
        spot = from_z.at[z]
        return remote(spot, spot, z_send.at[step - 1], z_recv.at[step - 1], z_peer(step)[1])

    for step in range(1, nz):
        z_copy(step).start()
    for step in range(1, nz):
        z_copy(step).wait_recv()
    summed = from_z[0].astype(jnp.float32)[0:piece, :]
    for other in range(1, nz):
        summed = summed + from_z[other].astype(jnp.float32)[0:piece, :]
    gathered[x, y, 0:piece, :] = (summed * scale).astype(jnp.bfloat16)
    if stored > piece:
        gathered[x, y, piece:stored, :] = jnp.zeros((stored - piece, 128), jnp.bfloat16)

    def gy_copy(step):
        spot = gathered.at[x, y]
        return remote(spot, spot, gy_send.at[step - 1], gy_recv.at[step - 1], y_peer(step)[1])

    for step in range(1, ny):
        gy_copy(step).start()
    for step in range(1, ny):
        gy_copy(step).wait_recv()

    def gx_copy(step):
        spot = gathered.at[x]
        return remote(spot, spot, gx_send.at[step - 1], gx_recv.at[step - 1], x_peer(step)[1])

    for step in range(1, nx):
        gx_copy(step).start()
    for step in range(1, nx):
        gx_copy(step).wait_recv()

    for px, py, low, high, source, target, first, last, lane in pieces:
        if source is not None:
            target[first:last, lane:lane + 128] = gathered[px, py, 0:piece, :].astype(jnp.float32)[low:high, :]

    for step in range(1, nx):
        x_copy(step).wait_send()
        gx_copy(step).wait_send()
    for step in range(1, ny):
        y_copy(step).wait_send()
        gy_copy(step).wait_send()
    for step in range(1, nz):
        z_copy(step).wait_send()


def weight_totals(joining, point, depth, scale, strip_count):
    nx, nz, ny = strip_layout(strip_count)
    piece = -(-1600 // (nx * ny) // 8) * 8
    stored = -(-piece // 16) * 16
    vmem = pl.BlockSpec(memory_space=pltpu.VMEM)
    dma = pltpu.SemaphoreType.DMA
    depth_shape = (16, depth.shape[0] * 128)
    shapes = [joining.shape, point.shape, depth_shape]
    a, b, c = pl.pallas_call(
        functools.partial(total_kernel, (nx, nz, ny), piece, stored, scale),
        name="weight_totals",
        out_shape=tuple(jax.ShapeDtypeStruct(shape, jnp.float32) for shape in shapes),
        in_specs=[vmem] * 3,
        out_specs=(vmem,) * 3,
        scratch_shapes=[
            pltpu.VMEM(depth_shape, jnp.float32),
            pltpu.VMEM((nx, ny, piece, 128), jnp.float32),
            pltpu.VMEM((nx, ny, stored, 128), jnp.bfloat16),
            pltpu.VMEM((max(nx - 1, 1), ny, stored, 128), jnp.bfloat16),
            pltpu.VMEM((2, ny, stored, 128), jnp.bfloat16),
            pltpu.VMEM((nz, stored, 128), jnp.bfloat16),
            pltpu.VMEM((nx, ny, stored, 128), jnp.bfloat16),
            dma((nx,)), dma((nx,)), dma((ny,)), dma((ny,)), dma((nz,)), dma((nz,)),
            dma((ny,)), dma((ny,)), dma((nx,)), dma((nx,)),
        ],
        compiler_params=pltpu.CompilerParams(
            collective_id=1, has_side_effects=True, vmem_limit_bytes=32 << 20
        ),
    )(joining, point, depth)
    return a, b, c[: depth.shape[1]]


def per_device(features, cotangent, depth_weight, point_weight, joining_weight, branch_mask):
    row_count, col_count, chan_count = features.shape
    strip_count = lax.axis_size("strip")
    pixel_scale = 1.0 / math.sqrt(row_count * col_count * strip_count)
    output, joining_part, point_part, depth_part = branch_step(
        features, cotangent, depth_weight, point_weight, joining_weight, branch_mask, strip_count
    )
    joining_total, point_total, depth_total = weight_totals(
        joining_part, point_part, depth_part, pixel_scale, strip_count
    )
    return (output, joining_total, point_total[None], depth_total[None])


def solution(mesh):
    placed = (
        P("strip", None, None),
        P("strip", None, "branch"),
        P("branch", None, None),
        P("branch", None, None),
        P("branch", None),
        P(),
    )
    return jax.shard_map(
        per_device,
        mesh=mesh,
        in_specs=placed,
        out_specs=(
            P("strip", None, "branch"),
            P("branch", None),
            P("branch", None, None),
            P("branch", None, None),
        ),
        check_vma=False,
    )
```
